32 devices in a mesh: ep: 16 (over z, x, core), tp: 2 (over y).
Axes of the slice: x: 2, y: 2, z: 4, core: 2. Of those that a mesh axis runs over, the one named last changes fastest.
Arguments:
- tokens: bfloat16 [2048, 2048], P('ep', 'tp'), may hold values from -6 to 6
- cotangent: bfloat16 [2048, 2048], P('ep', 'tp'), may hold values from -12 to 12
- route_weights: bfloat16 [2048, 8], P('ep'), may hold values from 0.049804688 to 0.59765625
- routes: int32 [2048, 8], P('ep'), may hold values from 0 to 15, all different within a row; in each aligned block of 128 rows (0 to 127, 128 to 255, ...) at most 96 rows name the same one
- grid_gate: bfloat16 [16, 768, 2048], P('ep', 'tp'), may hold values from -4 to 4
- latent_gate: bfloat16 [16, 768, 2048], P('ep', 'tp'), may hold values from -0.5 to 0.5
- scale_gate: float32 [16, 768], P('ep', 'tp'), may hold values from 0.006 to 0.02
- grid_up: bfloat16 [16, 768, 2048], P('ep', 'tp'), may hold values from -4 to 4
- latent_up: bfloat16 [16, 768, 2048], P('ep', 'tp'), may hold values from -0.5 to 0.5
- scale_up: float32 [16, 768], P('ep', 'tp'), may hold values from 0.006 to 0.02
- grid_down: bfloat16 [16, 768, 2048], P('ep', 'tp'), may hold values from -4 to 4
- latent_down: bfloat16 [16, 768, 2048], P('ep', 'tp'), may hold values from -0.5 to 0.5
- scale_down: float32 [16, 2048], P('ep'), may hold values from 0.006 to 0.02
Outputs:
- grad_latent_gate: float32 [16, 768, 2048], P('ep', 'tp')
- grad_latent_up: float32 [16, 768, 2048], P('ep', 'tp')
- grad_latent_down: float32 [16, 768, 2048], P('ep', 'tp')
- token_grad: bfloat16 [2048, 2048], P('ep', 'tp')
- route_grad: float32 [2048, 8], P('ep')
The draws below stay inside these ranges and needn't reach their ends.
Inputs may be any that keep to these rules, and one draw needn't show every extreme that they name: `routes`: each row names 8 different experts. In each aligned block of 128 tokens (the tokens of one index of ep), no expert is named by more than 96 of them, a bound that some block reaches.
All inputs are finite; a program needn't handle non-finite values.
Results may differ from the reference program's by a relative error of at most 0.006.
Values may be sent and summed in bfloat16 or wider, within the bound.
No kernel may reach another device: no remote copies, remote signals or barrier semaphores. Data moves between devices by JAX's collectives and lax.ppermute only.
A program may use at most 192 MiB of HBM per device.

```python
import math
import jax
import jax.numpy as jnp
import numpy as np
from jax import lax

D = 2048
FF = 768
TOP = 8
TOK_DEV = 128
EXPERTS = 16
CAP = 96
TOKENS = 2048


def block_levels(key, dims, cuts, least, top_value):
    def one(dim, shards_of):
        steps = jax.random.uniform(jax.random.fold_in(jax.random.fold_in(key, 6), dim), (shards_of,), jnp.float32, least / len(cuts), top_value / len(cuts))
        return jnp.repeat(jnp.exp(steps), dims[dim] // shards_of).reshape((-1,) + (1,) * (len(dims) - dim - 1))

    gain = one(*cuts[0])
    for cut in cuts[1:]:
        gain = gain * one(*cut)
    return gain


def deal_out(own_key, own, number, rows, count, top, bound, lean):
    order = jax.random.permutation(own_key, count)
    heavy_load, usual = portions_of(count, rows * top, bound, lean, True), portions_of(count, rows * top, bound, lean, False)
    places = jnp.arange(count)

    def named(lengths, turn):
        used = int((lengths > 0).sum())
        fixed = max(1, used // 4)
        passed = fixed + (places - fixed + turn * (used - fixed)) % max(1, count - fixed)
        return jnp.zeros((count,), jnp.int32).at[order[jnp.where(places < fixed, places, passed)]].set(jnp.asarray(lengths, jnp.int32))

    lengths = jnp.where(number % 4 == 0, named(heavy_load, number // 4), named(usual, number - number // 4 - 1))
    mixed = jax.random.permutation(jax.random.fold_in(own, 3), count)
    donor, sink = mixed[0:count // 2 * 2:2], mixed[1:count // 2 * 2:2]
    room = jnp.minimum(lengths[donor] - 1, bound - lengths[sink]) // 2
    room = jnp.where((donor == order[0]) | (sink == order[0]) | (lengths[sink] == 0), 0, jnp.maximum(room, 0))
    passed = jax.random.randint(jax.random.fold_in(own, 4), (count // 2,), 0, 1 << 20) % (room + 1)
    lengths = lengths.at[donor].add(-passed).at[sink].add(passed)
    items = jnp.searchsorted(jnp.cumsum(lengths), jnp.arange(rows * top), side="right").astype(jnp.int32)
    listing = items.reshape(top, rows).T
    listing = listing[jax.random.permutation(jax.random.fold_in(own, 1), rows)]
    turn = jax.random.randint(jax.random.fold_in(own, 2), (rows, 1), 0, top)
    return jnp.take_along_axis(listing, (jnp.arange(top)[None, :] + turn) % top, axis=1)


def portions_of(amount, total, bound, skew, full):
    loads = [(1 << 20) // math.isqrt(grade ** skew) + 1 for grade in range(1, amount + 1)]
    largest = bound if full else min(bound, max(-(-total // amount), total * loads[0] // sum(loads)))
    least = 1 if total - largest >= amount - 1 else 0
    counts, surplus = [largest] + [least] * (amount - 1), total - largest - least * (amount - 1)
    while surplus > 0:
        candidates = [i for i in range(1, amount) if counts[i] < largest] or [i for i in range(1, amount) if counts[i] < bound]
        mass, left = sum([loads[i] for i in candidates]), surplus
        for i in candidates:
            addition = min(bound - counts[i], max(1, left * loads[i] // mass), surplus)
            counts[i] = counts[i] + addition
            surplus = surplus - addition
    return np.array(counts)


def gaussian(own_key, extent, scale, limit, split=(), kind=jnp.bfloat16):
    level = block_levels(own_key, extent, split, -0.22, 0.18) if split else 1.0
    values = jax.random.normal(own_key, extent, jnp.float32) * scale * level
    return jnp.minimum(jnp.maximum(values, -limit), limit).astype(kind)


def setup_inputs(seed: int = 0) -> dict:
    arg_keys = jax.random.split(jax.random.key(seed), 14)
    tokens = gaussian(arg_keys[0], (TOKENS, D), 1.0, 6.0, ((0, 16), (1, 2)))
    cotangent = gaussian(arg_keys[1], (TOKENS, D), 2.0, 12.0, ((0, 16), (1, 2)))
    route_weights = jnp.clip(0.049804688 + 0.54785156 * jax.random.uniform(arg_keys[2], (TOKENS, TOP), jnp.float32) ** block_levels(arg_keys[2], (TOKENS, TOP), ((0, 16),), -0.2, 0.2), 0.049804688, 0.59765625).astype(jnp.bfloat16)
    routes_keys = jax.random.split(jax.random.fold_in(arg_keys[3], 1), TOKENS // TOK_DEV)
    routes_turns = jax.random.permutation(jax.random.fold_in(arg_keys[3], 3), TOKENS // TOK_DEV)
    routes = jax.vmap(lambda own, number: deal_out(jax.random.fold_in(arg_keys[3], 2), own, number, TOK_DEV, EXPERTS, TOP, CAP, 2))(routes_keys, routes_turns).reshape((TOKENS, TOP))
    grid_gate = gaussian(arg_keys[4], (EXPERTS, FF, D), 1.0, 4.0, ((0, 16), (1, 2)))
    latent_gate = jnp.clip(jax.random.uniform(arg_keys[5], (EXPERTS, FF, D), jnp.float32, -0.5, 0.5) * block_levels(arg_keys[5], (EXPERTS, FF, D), ((0, 16), (1, 2)), -0.4, 0.0), -0.5, 0.5).astype(jnp.bfloat16)
    scale_gate = jnp.clip(jnp.exp(math.log(0.02) - 1.2039728 * jax.random.uniform(arg_keys[6], (EXPERTS, FF), jnp.float32) ** block_levels(arg_keys[6], (EXPERTS, FF), ((0, 16), (1, 2)), -0.2, 0.2)), 0.006, 0.02)
    grid_up = gaussian(arg_keys[7], (EXPERTS, FF, D), 1.0, 4.0, ((0, 16), (1, 2)))
    latent_up = jnp.clip(jax.random.uniform(arg_keys[8], (EXPERTS, FF, D), jnp.float32, -0.5, 0.5) * block_levels(arg_keys[8], (EXPERTS, FF, D), ((0, 16), (1, 2)), -0.4, 0.0), -0.5, 0.5).astype(jnp.bfloat16)
    scale_up = jnp.clip(jnp.exp(math.log(0.02) - 1.2039728 * jax.random.uniform(arg_keys[9], (EXPERTS, FF), jnp.float32) ** block_levels(arg_keys[9], (EXPERTS, FF), ((0, 16), (1, 2)), -0.2, 0.2)), 0.006, 0.02)
    grid_down = gaussian(arg_keys[10], (EXPERTS, FF, D), 1.0, 4.0, ((0, 16), (1, 2)))
    latent_down = jnp.clip(jax.random.uniform(arg_keys[11], (EXPERTS, FF, D), jnp.float32, -0.5, 0.5) * block_levels(arg_keys[11], (EXPERTS, FF, D), ((0, 16), (1, 2)), -0.4, 0.0), -0.5, 0.5).astype(jnp.bfloat16)
    scale_down = jnp.clip(jnp.exp(math.log(0.02) - 1.2039728 * jax.random.uniform(arg_keys[12], (EXPERTS, D), jnp.float32) ** block_levels(arg_keys[12], (EXPERTS, D), ((0, 16),), -0.2, 0.2)), 0.006, 0.02)
    return {"tokens": tokens, "cotangent": cotangent, "route_weights": route_weights, "routes": routes, "grid_gate": grid_gate, "latent_gate": latent_gate, "scale_gate": scale_gate, "grid_up": grid_up, "latent_up": latent_up, "scale_up": scale_up, "grid_down": grid_down, "latent_down": latent_down, "scale_down": scale_down}


temper = 0.25
grad_factor = 8.0


def soften_rows(grid, latent, scale):
    level = grid.astype(jnp.float32) + 0.5 * (1.0 + jnp.tanh(latent.astype(jnp.float32) / temper))
    return level * scale[:, None]


def soften_cols(grid, latent, scale):
    level = grid.astype(jnp.float32) + 0.5 * (1.0 + jnp.tanh(latent.astype(jnp.float32) / temper))
    return level * scale[None, :]


def latent_rows(grad_weight, latent, scale):
    slope = jnp.tanh(latent.astype(jnp.float32) / temper)
    return grad_factor * grad_weight * scale[:, None] * (1.0 - slope * slope) / (2.0 * temper)


def latent_cols(grad_weight, latent, scale):
    slope = jnp.tanh(latent.astype(jnp.float32) / temper)
    return grad_factor * grad_weight * scale[None, :] * (1.0 - slope * slope) / (2.0 * temper)


def block_slots(block_routes, experts, capacity):
    flat = block_routes.reshape(-1).astype(jnp.int32)
    columns = jnp.arange(experts, dtype=jnp.int32)
    onehot = (flat[:, None] == columns[None, :]).astype(jnp.int32)
    earlier = jnp.cumsum(onehot, axis=0) - onehot
    return flat * capacity + jnp.sum(earlier * onehot, axis=1).astype(jnp.int32)


def entry_table(dest, entries, experts, capacity):
    table = jnp.full((experts * capacity,), entries, jnp.int32)
    return table.at[dest].set(jnp.arange(entries, dtype=jnp.int32))


def expert_backward(rows_x, rows_y, rows_p, w_gate, w_up, w_down):
    rowwise = (((1,), (1,)), ((), ()))
    gate = lax.dot_general(rows_x, w_gate, rowwise, preferred_element_type=jnp.float32)
    upper = lax.dot_general(rows_x, w_up, rowwise, preferred_element_type=jnp.float32)
    sigma = jax.nn.sigmoid(gate)
    active = gate * sigma
    hidden = active * upper
    weight = rows_p.astype(jnp.float32)[:, None]
    scaled = (hidden * weight).astype(jnp.bfloat16)
    back_hidden = lax.dot_general(rows_y, w_down, rowwise, preferred_element_type=jnp.float32)
    score = jnp.sum(hidden * back_hidden, axis=1)
    delta = back_hidden * weight
    grad_gate = (delta * upper * sigma * (1.0 + gate * (1.0 - sigma))).astype(jnp.bfloat16)
    grad_upper = (delta * active).astype(jnp.bfloat16)
    contract = (((0,), (0,)), ((), ()))
    grad_wg = lax.dot_general(grad_gate, rows_x, contract, preferred_element_type=jnp.float32)
    grad_wu = lax.dot_general(grad_upper, rows_x, contract, preferred_element_type=jnp.float32)
    grad_wd = lax.dot_general(scaled, rows_y, contract, preferred_element_type=jnp.float32)
    back_rows = jnp.dot(grad_gate, w_gate, preferred_element_type=jnp.float32)
    back_rows = back_rows + jnp.dot(grad_upper, w_up, preferred_element_type=jnp.float32)
    return grad_wg, grad_wu, grad_wd, back_rows, score


def reference(tokens, cotangent, route_weights, routes, grid_gate, latent_gate, scale_gate, grid_up, latent_up, scale_up, grid_down, latent_down, scale_down):
    blocks = TOKENS // TOK_DEV
    entries = TOK_DEV * TOP
    dest = jax.vmap(lambda r: block_slots(r, EXPERTS, CAP))(routes.reshape(blocks, TOK_DEV, TOP))
    local = jax.vmap(lambda d: entry_table(d, entries, EXPERTS, CAP))(dest)
    offsets = (jnp.arange(blocks, dtype=jnp.int32) * entries)[:, None]
    global_entry = jnp.where(local == entries, TOKENS * TOP, local + offsets).astype(jnp.int32)
    table = global_entry.reshape(blocks, EXPERTS, CAP).transpose(1, 0, 2).reshape(EXPERTS, blocks * CAP)
    tokens_pad = jnp.concatenate([tokens, jnp.zeros((1, D), jnp.bfloat16)], axis=0)
    cotan_pad = jnp.concatenate([cotangent, jnp.zeros((1, D), jnp.bfloat16)], axis=0)
    weights_pad = jnp.concatenate([route_weights.reshape(-1), jnp.zeros((1,), jnp.bfloat16)], axis=0)

    def step(carry, inputs):
        token_acc, score_acc = carry
        entry, g_grid, g_lat, g_scale, u_grid, u_lat, u_scale, d_grid, d_lat, d_scale = inputs
        token = (entry // TOP).astype(jnp.int32)
        rows_x = tokens_pad[token]
        rows_y = cotan_pad[token]
        rows_p = weights_pad[entry]
        w_gate = soften_rows(g_grid, g_lat, g_scale).astype(jnp.bfloat16)
        w_up = soften_rows(u_grid, u_lat, u_scale).astype(jnp.bfloat16)
        w_down = soften_cols(d_grid, d_lat, d_scale).astype(jnp.bfloat16)
        grad_wg, grad_wu, grad_wd, back_rows, score = expert_backward(rows_x, rows_y, rows_p, w_gate, w_up, w_down)
        token_acc = token_acc.at[token].add(back_rows)
        score_acc = score_acc.at[entry].add(score)
        outs = (latent_rows(grad_wg, g_lat, g_scale), latent_rows(grad_wu, u_lat, u_scale), latent_cols(grad_wd, d_lat, d_scale))
        return (token_acc, score_acc), outs

    start = (jnp.zeros((TOKENS + 1, D), jnp.float32), jnp.zeros((TOKENS * TOP + 1,), jnp.float32))
    inputs = (table, grid_gate, latent_gate, scale_gate, grid_up, latent_up, scale_up, grid_down, latent_down, scale_down)
    (token_acc, score_acc), (grad_gate, grad_upper, grad_lower) = lax.scan(step, start, inputs)
    token_grad = token_acc[:TOKENS].astype(jnp.bfloat16)
    route_grad = score_acc[:TOKENS * TOP].reshape(TOKENS, TOP)
    return grad_gate, grad_upper, grad_lower, token_grad, route_grad
```

```python
import functools

import jax
import jax.numpy as jnp
from jax import lax
from jax.experimental import pallas as pl
from jax.experimental.pallas import tpu as pltpu
from jax.sharding import PartitionSpec as P

temper = 0.25
grad_factor = 8.0


def soften_rows(grid, latent, scale):
    level = grid.astype(jnp.float32) + 0.5 * (1.0 + jnp.tanh(latent.astype(jnp.float32) / temper))
    return level * scale[:, None]


def soften_cols(grid, latent, scale):
    level = grid.astype(jnp.float32) + 0.5 * (1.0 + jnp.tanh(latent.astype(jnp.float32) / temper))
    return level * scale[None, :]


def latent_rows(grad_weight, latent, scale):
    slope = jnp.tanh(latent.astype(jnp.float32) / temper)
    return grad_factor * grad_weight * scale[:, None] * (1.0 - slope * slope) / (2.0 * temper)


def latent_cols(grad_weight, latent, scale):
    slope = jnp.tanh(latent.astype(jnp.float32) / temper)
    return grad_factor * grad_weight * scale[None, :] * (1.0 - slope * slope) / (2.0 * temper)


def block_slots(block_routes, experts, capacity):
    flat = block_routes.reshape(-1)
    columns = jnp.arange(experts, dtype=jnp.int32)
    onehot = (flat[:, None] == columns[None, :]).astype(jnp.int32)
    earlier = jnp.cumsum(onehot, axis=0) - onehot
    return flat * capacity + jnp.sum(earlier * onehot, axis=1)


def expert_backward(rows_x, rows_y, rows_p, w_gate, w_up, w_down):
    rowwise = (((1,), (1,)), ((), ()))
    gate = lax.dot_general(rows_x, w_gate, rowwise, preferred_element_type=jnp.float32)
    upper = lax.dot_general(rows_x, w_up, rowwise, preferred_element_type=jnp.float32)
    sigma = jax.nn.sigmoid(gate)
    active = gate * sigma
    hidden = active * upper
    weight = rows_p.astype(jnp.float32)[:, None]
    scaled = (hidden * weight).astype(jnp.bfloat16)
    back_hidden = lax.dot_general(rows_y, w_down, rowwise, preferred_element_type=jnp.float32)
    score = jnp.sum(hidden * back_hidden, axis=1)
    delta = back_hidden * weight
    grad_gate = (delta * upper * sigma * (1.0 + gate * (1.0 - sigma))).astype(jnp.bfloat16)
    grad_upper = (delta * active).astype(jnp.bfloat16)
    contract = (((0,), (0,)), ((), ()))
    grad_wg = lax.dot_general(grad_gate, rows_x, contract, preferred_element_type=jnp.float32)
    grad_wu = lax.dot_general(grad_upper, rows_x, contract, preferred_element_type=jnp.float32)
    grad_wd = lax.dot_general(scaled, rows_y, contract, preferred_element_type=jnp.float32)
    back_rows = jnp.dot(grad_gate, w_gate, preferred_element_type=jnp.float32)
    back_rows = back_rows + jnp.dot(grad_upper, w_up, preferred_element_type=jnp.float32)
    return (grad_wg, grad_wu, grad_wd, back_rows, score)


def pad_rows(values):
    return jnp.concatenate([values, jnp.zeros((1, values.shape[1]), values.dtype)], axis=0)


def routed_body(
    tokens,
    cotangent,
    route_weights,
    routes,
    grid_gate,
    latent_gate,
    scale_gate,
    grid_up,
    latent_up,
    scale_up,
    grid_down,
    latent_down,
    scale_down,
):
    n_ep = lax.axis_size("ep")
    experts = n_ep * grid_gate.shape[0]
    tok_rows, top = routes.shape
    capacity = min(tok_rows, 3 * tok_rows * top // (2 * experts))
    entries = tok_rows * top
    dest = block_slots(routes, experts, capacity)
    table = (
        jnp.full((experts * capacity,), entries, jnp.int32)
        .at[dest]
        .set(jnp.arange(entries, dtype=jnp.int32))
    )
    token_table = table // top
    weights_pad = jnp.concatenate(
        [route_weights.reshape(-1), jnp.zeros((1,), jnp.bfloat16)], axis=0
    )
    send_weights = weights_pad[table].reshape(experts, capacity)
    w_gate = soften_rows(grid_gate[0], latent_gate[0], scale_gate[0]).astype(jnp.bfloat16)
    w_up = soften_rows(grid_up[0], latent_up[0], scale_up[0]).astype(jnp.bfloat16)
    w_down = soften_cols(grid_down[0], latent_down[0], scale_down[0]).astype(jnp.bfloat16)
    part_x = pad_rows(tokens)[token_table].reshape(experts, capacity, -1)
    part_y = pad_rows(cotangent)[token_table].reshape(experts, capacity, -1)
    some_x, some_y, got_p = (
        lax.all_to_all(part_x, "ep", split_axis=0, concat_axis=0, tiled=True),
        lax.all_to_all(part_y, "ep", split_axis=0, concat_axis=0, tiled=True),
        lax.all_to_all(send_weights, "ep", split_axis=0, concat_axis=0, tiled=True),
    )
    got_x, got_y = (
        lax.all_gather(some_x, "tp", axis=2, tiled=True),
        lax.all_gather(some_y, "tp", axis=2, tiled=True),
    )
    width = got_x.shape[2]
    rows_x = got_x.reshape(-1, width)
    rows_y = got_y.reshape(-1, width)
    rows_p = got_p.reshape(-1)
    grad_wg, grad_wu, grad_wd, back_rows, score = expert_backward(
        rows_x, rows_y, rows_p, w_gate, w_up, w_down
    )
    grad_gate = latent_rows(grad_wg, latent_gate[0], scale_gate[0])[None]
    grad_upper = latent_rows(grad_wu, latent_up[0], scale_up[0])[None]
    grad_lower = latent_cols(grad_wd, latent_down[0], scale_down[0])[None]
    score = lax.psum(score.reshape(n_ep, capacity), "tp")
    back_rows = back_rows.reshape(n_ep, capacity, width)
    came_rows, came_score = (
        lax.all_to_all(back_rows, "ep", split_axis=0, concat_axis=0, tiled=True),
        lax.all_to_all(score, "ep", split_axis=0, concat_axis=0, tiled=True),
    )
    flat_rows = came_rows.reshape(experts * capacity, width)
    summed = jnp.sum(flat_rows[dest].reshape(tok_rows, top, width), axis=1)
    token_grad = lax.psum_scatter(summed, "tp", scatter_dimension=1, tiled=True).astype(
        jnp.bfloat16
    )
    route_grad = came_score.reshape(-1)[dest].reshape(tok_rows, top)
    return (grad_gate, grad_upper, grad_lower, token_grad, route_grad)


LANES = 128


def swap(value, ep_bits, tp_bits=0):
    n_ep, n_tp = lax.axis_size("ep"), lax.axis_size("tp")
    pairs = [
        (e * n_tp + t, (e ^ ep_bits) * n_tp + (t ^ tp_bits))
        for e in range(n_ep)
        for t in range(n_tp)
    ]
    return lax.ppermute(value, ("ep", "tp"), pairs)


PIECES = (
    ((0, 0, 0), (1, 0, 0)),
    ((0, 0, 1), (0, 1, 1)),
    ((0, 1, 0), (1, 1, 0)),
    ((1, 0, 1), (1, 1, 1)),
)


def piece_copies(pieces, buf, sems, tok_rows):
    part = tok_rows // 2
    copies = []
    for number, ref in enumerate(pieces):
        core = number // len(PIECES)
        for k, (x_bit, y_bit, upper) in enumerate(PIECES[number % len(PIECES)]):
            row = (core * 2 + x_bit) * tok_rows + upper * part
            copies.append(
                pltpu.make_async_copy(
                    ref.at[pl.ds(k * part, part), :],
                    buf.at[y_bit, pl.ds(row, part), :],
                    sems.at[2 * number + k],
                )
            )
    return copies


def nt(lhs, rhs):
    return lax.dot_general(lhs, rhs, (((1,), (1,)), ((), ())), preferred_element_type=jnp.float32)


def tn(lhs, rhs):
    return lax.dot_general(lhs, rhs, (((0,), (0,)), ((), ())), preferred_element_type=jnp.float32)


def group_kernel(tok_rows, width, where_ref, *refs):
    pieces, (wg_hbm, wu_hbm, wd_hbm) = refs[:8], refs[8:11]
    keep_ref, send_ref, dg_ref, du_ref, ap_ref = refs[11:16]
    buf, wg, wu, wd, gate_s, up_s, back_s, sems, wsems = refs[16:]
    expert, mine = where_ref[0], where_ref[1]
    data = piece_copies(pieces, buf, sems, tok_rows)
    loads = []
    for i, (src, dst) in enumerate(((wg_hbm, wg), (wu_hbm, wu), (wd_hbm, wd))):
        for y_bit in range(2):
            cols = pl.multiple_of(jnp.bitwise_xor(mine, y_bit) * width, LANES)
            loads.append(
                pltpu.make_async_copy(
                    src.at[:, pl.ds(cols, width)], dst.at[y_bit], wsems.at[2 * i + y_bit]
                )
            )
    for copy in data + loads:
        copy.start()
    for copy in data + loads:
        copy.wait()
    x_cols, y_cols = pl.ds(0, width), pl.ds(width + LANES, width)
    gate_s[...] = nt(buf[0, :, x_cols], wg[0]) + nt(buf[1, :, x_cols], wg[1])
    up_s[...] = nt(buf[0, :, x_cols], wu[0]) + nt(buf[1, :, x_cols], wu[1])
    back_s[...] = nt(buf[0, :, y_cols], wd[0]) + nt(buf[1, :, y_cols], wd[1])
    chunk = tok_rows // 2
    out_rows = tok_rows

    for i in range(buf.shape[1] // chunk):
        rows = pl.ds(i * chunk, chunk)
        gate, upper, back = gate_s[rows, :], up_s[rows, :], back_s[rows, :]
        lane = lax.broadcasted_iota(jnp.int32, (chunk, LANES), 1)
        chosen = lane == expert
        dense = buf[0, rows, pl.ds(width, LANES)].astype(jnp.float32)
        weight = jnp.sum(jnp.where(chosen, dense, 0.0), axis=1, keepdims=True)
        sigma = jax.nn.sigmoid(gate)
        active = gate * sigma
        hidden = active * upper
        score = jnp.sum(hidden * back, axis=1, keepdims=True)
        delta = back * weight
        ap_ref[rows, :] = (hidden * weight).astype(jnp.bfloat16)
        dg_ref[rows, :] = (delta * upper * sigma * (1.0 + gate * (1.0 - sigma))).astype(jnp.bfloat16)
        du_ref[rows, :] = (delta * active).astype(jnp.bfloat16)
        spread = jnp.where(chosen, score, 0.0).astype(jnp.bfloat16)
        block, row = divmod(i * chunk, out_rows)
        core, x_bit = divmod(block, 2)
        for y_bit in range(2):
            out = send_ref if core else keep_ref
            out[2 * x_bit + y_bit, pl.ds(row, chunk), pl.ds(width, LANES)] = spread
    for y_bit in range(2):
        rows_back = jnp.dot(dg_ref[...], wg[y_bit], preferred_element_type=jnp.float32)
        rows_back = rows_back + jnp.dot(du_ref[...], wu[y_bit], preferred_element_type=jnp.float32)
        rows_back = rows_back.astype(jnp.bfloat16)
        for block in range(4):
            core, x_bit = divmod(block, 2)
            out = send_ref if core else keep_ref
            out[2 * x_bit + y_bit, :, pl.ds(0, width)] = rows_back[
                block * out_rows : (block + 1) * out_rows
            ]


def group_call(where, pieces, w_gate, w_up, w_down):
    two_rows, cols = pieces[0].shape
    tok_rows = two_rows
    hid, feat = w_gate.shape
    width = feat // 2
    rows = 4 * tok_rows
    anywhere = pl.BlockSpec(memory_space=pl.ANY)
    vmem = pl.BlockSpec(memory_space=pltpu.VMEM)
    out = jax.ShapeDtypeStruct((4, tok_rows, width + LANES), jnp.bfloat16)
    small = jax.ShapeDtypeStruct((rows, hid), jnp.bfloat16)
    return pl.pallas_call(
        functools.partial(group_kernel, tok_rows, width),
        out_shape=(out, out, small, small, small),
        in_specs=[pl.BlockSpec(memory_space=pltpu.SMEM)] + [anywhere] * 11,
        out_specs=(vmem,) * 5,
        scratch_shapes=[
            pltpu.VMEM((2, rows, cols), jnp.bfloat16),
            pltpu.VMEM((2, hid, width), jnp.bfloat16),
            pltpu.VMEM((2, hid, width), jnp.bfloat16),
            pltpu.VMEM((2, hid, width), jnp.bfloat16),
            pltpu.VMEM((rows, hid), jnp.float32),
            pltpu.VMEM((rows, hid), jnp.float32),
            pltpu.VMEM((rows, hid), jnp.float32),
            pltpu.SemaphoreType.DMA((16,)),
            pltpu.SemaphoreType.DMA((6,)),
        ],
        cost_estimate=pl.CostEstimate(
            flops=10 * rows * hid * feat, transcendentals=rows * hid, bytes_accessed=2 * 2 * rows * cols * 2
        ),
        name="expert_rows",
    )(where, *pieces, w_gate, w_up, w_down)


def grads_kernel(groups, tok_rows, width, where_ref, *refs):
    per = 11
    ins = refs[: groups * per]
    factors = refs[groups * per : groups * per + 3]
    outs = refs[groups * per + 3 : groups * per + 6]
    bufs, deltas, facs, accs, sems, dsems, fsems, osems = refs[groups * per + 6 :]
    mine = where_ref[1]
    x_cols, y_cols = pl.ds(0, width), pl.ds(width + LANES, width)

    def loads(g):
        refs_g = ins[g * per : (g + 1) * per]
        slot = g % 2
        copies = piece_copies(refs_g[:8], bufs.at[slot], sems.at[slot], tok_rows)
        for i in range(3):
            copies.append(
                pltpu.make_async_copy(refs_g[8 + i], deltas.at[slot, i], dsems.at[slot, i])
            )
        return copies

    fac_copies = [pltpu.make_async_copy(factors[i], facs.at[i], fsems.at[i]) for i in range(3)]
    current = loads(0)
    for copy in current:
        copy.start()
    for g in range(groups):
        following = loads(g + 1) if g + 1 < groups else fac_copies
        for copy in following:
            copy.start()
        for copy in current:
            copy.wait()
        slot = g % 2
        for i in range(3):
            cols = y_cols if i == 2 else x_cols
            for y_bit in range(2):
                part = tn(deltas[slot, i], bufs[slot, y_bit, :, cols])
                if g == 0:
                    accs[i, y_bit] = part
                else:
                    accs[i, y_bit] += part
        current = following
    for copy in current:
        copy.wait()
    writes = []
    for i in range(3):
        for y_bit in range(2):
            cols = pl.ds(pl.multiple_of(jnp.bitwise_xor(mine, y_bit) * width, LANES), width)
            accs[i, y_bit] = accs[i, y_bit] * facs[i, :, cols]
            copy = pltpu.make_async_copy(
                accs.at[i, y_bit], outs[i].at[:, cols], osems.at[2 * i + y_bit]
            )
            copy.start()
            writes.append(copy)
    for copy in writes:
        copy.wait()


def grads_call(where, group_inputs, factors):
    groups = len(group_inputs)
    tok_rows, cols = group_inputs[0][0].shape
    rows, hid = group_inputs[0][8].shape
    feat = factors[0].shape[1]
    width = feat // 2
    anywhere = pl.BlockSpec(memory_space=pl.ANY)
    out = jax.ShapeDtypeStruct((hid, feat), jnp.float32)
    flat = [ref for group in group_inputs for ref in group]
    return pl.pallas_call(
        functools.partial(grads_kernel, groups, tok_rows, width),
        out_shape=(out, out, out),
        in_specs=[pl.BlockSpec(memory_space=pltpu.SMEM)] + [anywhere] * (len(flat) + 3),
        out_specs=(anywhere,) * 3,
        scratch_shapes=[
            pltpu.VMEM((2, 2, rows, cols), jnp.bfloat16),
            pltpu.VMEM((2, 3, rows, hid), jnp.bfloat16),
            pltpu.VMEM((3, hid, feat), jnp.float32),
            pltpu.VMEM((3, 2, hid, width), jnp.float32),
            pltpu.SemaphoreType.DMA((2, 16)),
            pltpu.SemaphoreType.DMA((2, 3)),
            pltpu.SemaphoreType.DMA((3,)),
            pltpu.SemaphoreType.DMA((6,)),
        ],
        cost_estimate=pl.CostEstimate(
            flops=6 * groups * rows * hid * feat,
            transcendentals=0,
            bytes_accessed=groups * 2 * rows * cols * 2 + 6 * hid * feat * 4,
        ),
        name="latent_grads",
    )(where, *flat, *factors)


def factor_rows(latent, scale):
    slope = jnp.tanh(latent.astype(jnp.float32) / temper)
    return (grad_factor / (2.0 * temper)) * scale[:, None] * (1.0 - slope * slope)


def factor_cols(latent, scale):
    slope = jnp.tanh(latent.astype(jnp.float32) / temper)
    return (grad_factor / (2.0 * temper)) * scale[None, :] * (1.0 - slope * slope)


def plane_gather(block):
    half = block.shape[0] // 2
    low, high = block[:half], block[half:]
    low_x, high_y = swap(low, 2), swap(high, 0, 1)
    lows = jnp.concatenate([low, low_x], axis=0)
    highs = jnp.concatenate([high, high_y], axis=0)
    own = [lows, highs, swap(lows, 0, 1), swap(highs, 2)]
    return own + [swap(piece, 1) for piece in own]


def dense_body(
    tokens,
    cotangent,
    route_weights,
    routes,
    grid_gate,
    latent_gate,
    scale_gate,
    grid_up,
    latent_up,
    scale_up,
    grid_down,
    latent_down,
    scale_down,
):
    n_ep = lax.axis_size("ep")
    tok_rows, width = tokens.shape
    where = jnp.stack([lax.axis_index("ep"), lax.axis_index("tp")]).astype(jnp.int32)
    columns = jnp.arange(LANES, dtype=jnp.int32)
    onehot = routes[:, :, None] == columns[None, None, :]
    dense = jnp.sum(
        jnp.where(onehot, route_weights.astype(jnp.float32)[:, :, None], 0.0), axis=1
    ).astype(jnp.bfloat16)
    block = jnp.concatenate([tokens, dense, cotangent], axis=1)
    hops = list(range(0, n_ep, 4))
    blocks = [block if hop == 0 else swap(block, hop) for hop in hops]
    w_gate = soften_rows(grid_gate[0], latent_gate[0], scale_gate[0]).astype(jnp.bfloat16)
    w_up = soften_rows(grid_up[0], latent_up[0], scale_up[0]).astype(jnp.bfloat16)
    w_down = soften_cols(grid_down[0], latent_down[0], scale_down[0]).astype(jnp.bfloat16)
    factors = (
        factor_rows(latent_gate[0], scale_gate[0]),
        factor_rows(latent_up[0], scale_up[0]),
        factor_cols(latent_down[0], scale_down[0]),
    )
    group_inputs, total = [], None
    for hop, arrived in zip(hops, blocks):
        pieces = plane_gather(arrived)
        keep, send, dg, du, ap = group_call(where, pieces, w_gate, w_up, w_down)
        group_inputs.append([*pieces, dg, du, ap])
        both = keep.astype(jnp.float32) + swap(send, 1).astype(jnp.float32)
        out = both.astype(jnp.bfloat16)
        plane = (
            both[0]
            + swap(out[1], 0, 1).astype(jnp.float32)
            + swap(out[2], 2).astype(jnp.float32)
            + swap(out[3], 2, 1).astype(jnp.float32)
        )
        if hop:
            plane = swap(plane.astype(jnp.bfloat16), hop).astype(jnp.float32)
        total = plane if total is None else total + plane
    grads = grads_call(where, group_inputs, factors)
    token_grad = total[:, :width].astype(jnp.bfloat16)
    route_grad = jnp.sum(jnp.where(onehot, total[:, None, width:], 0.0), axis=2)
    return (grads[0][None], grads[1][None], grads[2][None], token_grad, route_grad)


def body_of(mesh):
    n_ep, n_tp = mesh.shape["ep"], mesh.shape["tp"]

    def body(tokens, cotangent, route_weights, routes, *weights):
        experts = n_ep * weights[0].shape[0]
        fits = n_tp == 2 and n_ep % 4 == 0 and (n_ep & (n_ep - 1)) == 0
        fits = fits and weights[0].shape[0] == 1 and experts <= LANES
        if fits and 2 * routes.shape[1] >= experts:
            return dense_body(tokens, cotangent, route_weights, routes, *weights)
        return routed_body(tokens, cotangent, route_weights, routes, *weights)

    return body


def solution(mesh):
    return jax.shard_map(
        body_of(mesh),
        mesh=mesh,
        in_specs=(
            P("ep", "tp"),
            P("ep", "tp"),
            P("ep", None),
            P("ep", None),
            P("ep", "tp", None),
            P("ep", "tp", None),
            P("ep", "tp"),
            P("ep", "tp", None),
            P("ep", "tp", None),
            P("ep", "tp"),
            P("ep", "tp", None),
            P("ep", "tp", None),
            P("ep", None),
        ),
        out_specs=(
            P("ep", "tp", None),
            P("ep", "tp", None),
            P("ep", "tp", None),
            P("ep", "tp"),
            P("ep", None),
        ),
        check_vma=False,
    )
```

```python
import functools

import jax
import jax.numpy as jnp
from jax import lax
from jax.experimental import pallas as pl
from jax.experimental.pallas import tpu as pltpu
from jax.sharding import PartitionSpec as P


temper = 0.25
grad_factor = 8.0


def soften_rows(grid, latent, scale):
    level = grid.astype(jnp.float32) + 0.5 * (1.0 + jnp.tanh(latent.astype(jnp.float32) / temper))
    return level * scale[:, None]


def soften_cols(grid, latent, scale):
    level = grid.astype(jnp.float32) + 0.5 * (1.0 + jnp.tanh(latent.astype(jnp.float32) / temper))
    return level * scale[None, :]


def latent_rows(grad_weight, latent, scale):
    slope = jnp.tanh(latent.astype(jnp.float32) / temper)
    return grad_factor * grad_weight * scale[:, None] * (1.0 - slope * slope) / (2.0 * temper)


def latent_cols(grad_weight, latent, scale):
    slope = jnp.tanh(latent.astype(jnp.float32) / temper)
    return grad_factor * grad_weight * scale[None, :] * (1.0 - slope * slope) / (2.0 * temper)


def block_slots(block_routes, experts, capacity):
    flat = block_routes.reshape(-1)
    columns = jnp.arange(experts, dtype=jnp.int32)
    onehot = (flat[:, None] == columns[None, :]).astype(jnp.int32)
    earlier = jnp.cumsum(onehot, axis=0) - onehot
    return flat * capacity + jnp.sum(earlier * onehot, axis=1)


def expert_backward(rows_x, rows_y, rows_p, w_gate, w_up, w_down):
    rowwise = (((1,), (1,)), ((), ()))
    gate = lax.dot_general(rows_x, w_gate, rowwise, preferred_element_type=jnp.float32)
    upper = lax.dot_general(rows_x, w_up, rowwise, preferred_element_type=jnp.float32)
    sigma = jax.nn.sigmoid(gate)
    active = gate * sigma
    hidden = active * upper
    weight = rows_p.astype(jnp.float32)[:, None]
    scaled = (hidden * weight).astype(jnp.bfloat16)
    back_hidden = lax.dot_general(rows_y, w_down, rowwise, preferred_element_type=jnp.float32)
    score = jnp.sum(hidden * back_hidden, axis=1)
    delta = back_hidden * weight
    grad_gate = (delta * upper * sigma * (1.0 + gate * (1.0 - sigma))).astype(jnp.bfloat16)
    grad_upper = (delta * active).astype(jnp.bfloat16)
    contract = (((0,), (0,)), ((), ()))
    grad_wg = lax.dot_general(grad_gate, rows_x, contract, preferred_element_type=jnp.float32)
    grad_wu = lax.dot_general(grad_upper, rows_x, contract, preferred_element_type=jnp.float32)
    grad_wd = lax.dot_general(scaled, rows_y, contract, preferred_element_type=jnp.float32)
    back_rows = jnp.dot(grad_gate, w_gate, preferred_element_type=jnp.float32)
    back_rows = back_rows + jnp.dot(grad_upper, w_up, preferred_element_type=jnp.float32)
    return (grad_wg, grad_wu, grad_wd, back_rows, score)


def pad_rows(values):
    return jnp.concatenate([values, jnp.zeros((1, values.shape[1]), values.dtype)], axis=0)


def routed_body(
    tokens,
    cotangent,
    route_weights,
    routes,
    grid_gate,
    latent_gate,
    scale_gate,
    grid_up,
    latent_up,
    scale_up,
    grid_down,
    latent_down,
    scale_down,
):
    n_ep = lax.axis_size("ep")
    experts = n_ep * grid_gate.shape[0]
    tok_rows, top = routes.shape
    capacity = min(tok_rows, 3 * tok_rows * top // (2 * experts))
    entries = tok_rows * top
    dest = block_slots(routes, experts, capacity)
    table = (
        jnp.full((experts * capacity,), entries, jnp.int32)
        .at[dest]
        .set(jnp.arange(entries, dtype=jnp.int32))
    )
    token_table = table // top
    weights_pad = jnp.concatenate(
        [route_weights.reshape(-1), jnp.zeros((1,), jnp.bfloat16)], axis=0
    )
    send_weights = weights_pad[table].reshape(experts, capacity)
    w_gate = soften_rows(grid_gate[0], latent_gate[0], scale_gate[0]).astype(jnp.bfloat16)
    w_up = soften_rows(grid_up[0], latent_up[0], scale_up[0]).astype(jnp.bfloat16)
    w_down = soften_cols(grid_down[0], latent_down[0], scale_down[0]).astype(jnp.bfloat16)
    part_x = pad_rows(tokens)[token_table].reshape(experts, capacity, -1)
    part_y = pad_rows(cotangent)[token_table].reshape(experts, capacity, -1)
    some_x, some_y, got_p = (
        lax.all_to_all(part_x, "ep", split_axis=0, concat_axis=0, tiled=True),
        lax.all_to_all(part_y, "ep", split_axis=0, concat_axis=0, tiled=True),
        lax.all_to_all(send_weights, "ep", split_axis=0, concat_axis=0, tiled=True),
    )
    got_x, got_y = (
        lax.all_gather(some_x, "tp", axis=2, tiled=True),
        lax.all_gather(some_y, "tp", axis=2, tiled=True),
    )
    width = got_x.shape[2]
    rows_x = got_x.reshape(-1, width)
    rows_y = got_y.reshape(-1, width)
    rows_p = got_p.reshape(-1)
    grad_wg, grad_wu, grad_wd, back_rows, score = expert_backward(
        rows_x, rows_y, rows_p, w_gate, w_up, w_down
    )
    grad_gate = latent_rows(grad_wg, latent_gate[0], scale_gate[0])[None]
    grad_upper = latent_rows(grad_wu, latent_up[0], scale_up[0])[None]
    grad_lower = latent_cols(grad_wd, latent_down[0], scale_down[0])[None]
    score = lax.psum(score.reshape(n_ep, capacity), "tp")
    back_rows = back_rows.reshape(n_ep, capacity, width)
    came_rows, came_score = (
        lax.all_to_all(back_rows, "ep", split_axis=0, concat_axis=0, tiled=True),
        lax.all_to_all(score, "ep", split_axis=0, concat_axis=0, tiled=True),
    )
    flat_rows = came_rows.reshape(experts * capacity, width)
    summed = jnp.sum(flat_rows[dest].reshape(tok_rows, top, width), axis=1)
    token_grad = lax.psum_scatter(summed, "tp", scatter_dimension=1, tiled=True).astype(
        jnp.bfloat16
    )
    route_grad = came_score.reshape(-1)[dest].reshape(tok_rows, top)
    return (grad_gate, grad_upper, grad_lower, token_grad, route_grad)


LANES = 128


def swap(value, ep_bits, tp_bits=0):
    n_ep, n_tp = lax.axis_size("ep"), lax.axis_size("tp")
    pairs = [
        (e * n_tp + t, (e ^ ep_bits) * n_tp + (t ^ tp_bits))
        for e in range(n_ep)
        for t in range(n_tp)
    ]
    return lax.ppermute(value, ("ep", "tp"), pairs)


PIECES = (
    (0, 0, 0),
    (1, 0, 0),
    (0, 1, 0),
    (1, 1, 0),
    (0, 0, 1),
    (0, 1, 1),
    (1, 0, 1),
    (1, 1, 1),
)


def stacked(pieces, y_bit, cols):
    parts = []
    for core in range(2):
        for x_bit in range(2):
            for upper in range(2):
                number = core * len(PIECES) + PIECES.index((x_bit, y_bit, upper))
                parts.append(pieces[number][:, cols])
    return parts


def nt(lhs, rhs):
    return lax.dot_general(lhs, rhs, (((1,), (1,)), ((), ())), preferred_element_type=jnp.float32)


def group_kernel(tok_rows, width, where_ref, *refs):
    pieces, weights = refs[:16], refs[16:22]
    outs, (deltas_ref, hid_ref) = refs[22:24], refs[24:26]
    both_s, back_s, weight_s = refs[26:]
    expert = where_ref[0]
    hid = hid_ref.shape[1]
    x_cols, y_cols = pl.ds(LANES, width), pl.ds(LANES + width, width)

    def whole(cols):
        halves = [jnp.concatenate(stacked(pieces, y_bit, cols), axis=0) for y_bit in range(2)]
        return jnp.concatenate(halves, axis=1)

    def weight_rows(i):
        return jnp.concatenate([weights[2 * i][...], weights[2 * i + 1][...]], axis=1)

    both_s[...] = nt(whole(x_cols), jnp.concatenate([weight_rows(0), weight_rows(1)], axis=0))
    back_s[...] = nt(whole(y_cols), weight_rows(2))
    part = tok_rows // 2
    for i, dense in enumerate(stacked(pieces, 0, pl.ds(0, LANES))):
        lane = lax.broadcasted_iota(jnp.int32, dense.shape, 1)
        weight_s[i * part : (i + 1) * part] = jnp.sum(
            jnp.where(lane == expert, dense.astype(jnp.float32), 0.0), axis=1, keepdims=True
        )
    chunk = tok_rows // 4
    for i in range(both_s.shape[0] // chunk):
        rows = pl.ds(i * chunk, chunk)
        gate, upper, back = both_s[rows, :hid], both_s[rows, hid:], back_s[rows, :]
        weight = weight_s[rows]
        sigma = jax.nn.sigmoid(gate)
        active = gate * sigma
        hidden = active * upper
        score = jnp.sum(hidden * back, axis=1, keepdims=True)
        delta = back * weight
        deltas_ref[rows, :hid] = (
            delta * upper * sigma * (1.0 + gate * (1.0 - sigma))
        ).astype(jnp.bfloat16)
        deltas_ref[rows, hid:] = (delta * active).astype(jnp.bfloat16)
        hid_ref[rows, :] = (hidden * weight).astype(jnp.bfloat16)
        lane = lax.broadcasted_iota(jnp.int32, (chunk, LANES), 1)
        spread = jnp.where(lane == expert, score, 0.0).astype(jnp.bfloat16)
        block, row = divmod(i * chunk, tok_rows)
        core, x_bit = divmod(block, 2)
        for y_bit in range(2):
            outs[core][y_bit, x_bit, pl.ds(row, chunk), pl.ds(width, LANES)] = spread
    for y_bit in range(2):
        both = jnp.concatenate([weights[y_bit][...], weights[2 + y_bit][...]], axis=0)
        rows_back = jnp.dot(deltas_ref[...], both, preferred_element_type=jnp.float32)
        rows_back = rows_back.astype(jnp.bfloat16)
        for block in range(4):
            core, x_bit = divmod(block, 2)
            outs[core][y_bit, x_bit, :, pl.ds(0, width)] = rows_back[
                block * tok_rows : (block + 1) * tok_rows
            ]


VMEM_WHOLE = pl.BlockSpec(memory_space=pltpu.VMEM)
SMEM_WHOLE = pl.BlockSpec(memory_space=pltpu.SMEM)
HBM_WHOLE = pl.BlockSpec(memory_space=pltpu.HBM)


def away(values):
    return [pltpu.with_memory_space_constraint(value, pltpu.HBM) for value in values]


def near(values):
    return [pltpu.with_memory_space_constraint(value, pltpu.VMEM) for value in values]


def group_call(where, pieces, weights):
    tok_rows = 2 * pieces[0].shape[0]
    hid, width = weights[0].shape
    rows = 4 * tok_rows
    out = pltpu.VMEM((2, 2, tok_rows, width + LANES), jnp.bfloat16)
    return pl.pallas_call(
        functools.partial(group_kernel, tok_rows, width),
        out_shape=(
            out,
            out,
            pltpu.VMEM((rows, 2 * hid), jnp.bfloat16),
            pltpu.VMEM((rows, hid), jnp.bfloat16),
        ),
        in_specs=[SMEM_WHOLE] + [VMEM_WHOLE] * 22,
        out_specs=(VMEM_WHOLE,) * 4,
        scratch_shapes=[
            pltpu.VMEM((rows, 2 * hid), jnp.float32),
            pltpu.VMEM((rows, hid), jnp.float32),
            pltpu.VMEM((rows, 1), jnp.float32),
        ],
        cost_estimate=pl.CostEstimate(
            flops=20 * rows * hid * width, transcendentals=rows * hid, bytes_accessed=2 * 4 * rows * width * 2
        ),
        compiler_params=pltpu.CompilerParams(vmem_limit_bytes=12 * 2**20),
        name="expert_rows",
    )(where, *near(pieces), *near(weights))


def core_kernel(keep_ref, got_ref, own_ref, y_ref, x_ref, far_ref):
    for (y_bit, x_bit), ref in (((1, 0), y_ref), ((0, 1), x_ref), ((1, 1), far_ref), ((0, 0), own_ref)):
        total = keep_ref[y_bit, x_bit].astype(jnp.float32) + got_ref[y_bit, x_bit].astype(jnp.float32)
        ref[...] = total.astype(ref.dtype)


def core_call(keep, got):
    shape = keep.shape[2:]
    sent = pltpu.VMEM(shape, jnp.bfloat16)
    return pl.pallas_call(
        core_kernel,
        out_shape=(pltpu.VMEM(shape, jnp.float32), sent, sent, sent),
        in_specs=[VMEM_WHOLE] * 2,
        out_specs=(VMEM_WHOLE,) * 4,
        compiler_params=pltpu.CompilerParams(vmem_limit_bytes=4 * 2**20),
        name="core_sum",
    )(*near((keep, got)))


def plane_kernel(own_ref, y_ref, x_ref, far_ref, out_ref):
    total = own_ref[...] + y_ref[...].astype(jnp.float32)
    total = total + x_ref[...].astype(jnp.float32) + far_ref[...].astype(jnp.float32)
    out_ref[...] = total.astype(out_ref.dtype)


def plane_call(own, from_y, from_x, from_far, dtype):
    return pl.pallas_call(
        plane_kernel,
        out_shape=pltpu.VMEM(own.shape, dtype),
        in_specs=[VMEM_WHOLE] * 4,
        out_specs=VMEM_WHOLE,
        compiler_params=pltpu.CompilerParams(vmem_limit_bytes=4 * 2**20),
        name="plane_sum",
    )(*near((own, from_y, from_x, from_far)))


def weight_sums_kernel(first, width, *refs):
    deltas_ref, hid_ref, pieces = refs[0], refs[1], refs[2:18]
    sums = refs[18:20] if first else refs[20:22]
    flipped = refs[-1]
    count = deltas_ref.shape[1]
    flipped[:count] = deltas_ref[...].T
    flipped[count:] = hid_ref[...].T
    tile = width // 2
    for rows, start, out in (
        (pl.ds(0, count), LANES, sums[0]),
        (pl.ds(count, hid_ref.shape[1]), LANES + width, sums[1]),
    ):
        for y_bit in range(2):
            for t in range(2):
                data = jnp.concatenate(stacked(pieces, y_bit, pl.ds(start + t * tile, tile)), axis=0)
                part = jnp.dot(flipped[rows], data, preferred_element_type=jnp.float32)
                here = pl.ds(y_bit * width + t * tile, tile)
                out[:, here] = part if first else out[:, here] + part


def weight_sums_call(deltas, hidden, pieces, sums):
    rows, count = deltas.shape
    hid, width = hidden.shape[1], (pieces[0].shape[1] - LANES) // 2
    first = sums is None
    outs = (pltpu.VMEM((count, 2 * width), jnp.float32), pltpu.VMEM((hid, 2 * width), jnp.float32))
    held = () if first else tuple(near(sums))
    return pl.pallas_call(
        functools.partial(weight_sums_kernel, first, width),
        out_shape=outs,
        in_specs=[VMEM_WHOLE] * (18 + len(held)),
        out_specs=(VMEM_WHOLE,) * 2,
        scratch_shapes=[pltpu.VMEM((count + hid, rows), jnp.bfloat16)],
        input_output_aliases={} if first else {18: 0, 19: 1},
        compiler_params=pltpu.CompilerParams(vmem_limit_bytes=8 * 2**20),
        cost_estimate=pl.CostEstimate(
            flops=4 * (count + hid) * rows * width, transcendentals=0, bytes_accessed=4 * rows * width * 2
        ),
        name="weight_sums",
    )(*near((deltas, hidden)), *near(pieces), *held)


def grads_kernel(where_ref, *refs):
    sums, latents, scales, outs = refs[0:2], refs[2:5], refs[5:8], refs[8:11]
    lats, stage, lsems, osems = refs[11:]
    mine = where_ref[1]
    slots = stage.shape[0]
    hid, feat = latents[0].shape
    width, tile = feat // 2, stage.shape[2]
    lat_copies = [pltpu.make_async_copy(latents[i], lats.at[i], lsems.at[i]) for i in range(3)]
    for copy in lat_copies:
        copy.start()
    writes = []
    for i in range(3):
        lat_copies[i].wait()
        for y_bit in range(2):
            for t in range(width // tile):
                there = jnp.bitwise_xor(mine, y_bit) * width + t * tile
                there = pl.ds(pl.multiple_of(there, LANES), tile)
                here = pl.ds(y_bit * width + t * tile, tile)
                slope = jnp.tanh(lats[i, :, there].astype(jnp.float32) / temper)
                scale = scales[i][:, there] if i == 2 else scales[i][...]
                factor = (grad_factor / (2.0 * temper)) * scale * (1.0 - slope * slope)
                total = sums[1][:, here] if i == 2 else sums[0][pl.ds(i * hid, hid), here]
                slot = len(writes) % slots
                if len(writes) >= slots:
                    writes[len(writes) - slots].wait()
                stage[slot] = total * factor
                copy = pltpu.make_async_copy(stage.at[slot], outs[i].at[:, there], osems.at[slot])
                copy.start()
                writes.append(copy)
    for copy in writes[-slots:]:
        copy.wait()


def grads_call(where, sums, latents, scales):
    hid, feat = latents[0].shape
    out = jax.ShapeDtypeStruct((hid, feat), jnp.float32)
    return pl.pallas_call(
        grads_kernel,
        out_shape=(out,) * 3,
        in_specs=[SMEM_WHOLE] + [VMEM_WHOLE] * 2 + [HBM_WHOLE] * 3 + [VMEM_WHOLE] * 3,
        out_specs=(HBM_WHOLE,) * 3,
        scratch_shapes=[
            pltpu.VMEM((3, hid, feat), jnp.bfloat16),
            pltpu.VMEM((6, hid, feat // 4), jnp.float32),
            pltpu.SemaphoreType.DMA((3,)),
            pltpu.SemaphoreType.DMA((6,)),
        ],
        compiler_params=pltpu.CompilerParams(vmem_limit_bytes=12 * 2**20),
        cost_estimate=pl.CostEstimate(
            flops=18 * hid * feat,
            transcendentals=3 * hid * feat,
            bytes_accessed=3 * hid * feat * 6,
        ),
        name="latent_grads",
    )(where, *near(sums), *away(latents), *scales)


def pack_kernel(routes_ref, weights_ref, x_hbm, y_hbm, low_ref, high_ref, sems):
    tok_rows, width = x_hbm.shape
    half = tok_rows // 2
    copies = []
    for i, ref in enumerate((low_ref, high_ref)):
        for k, src in enumerate((x_hbm, y_hbm)):
            copies.append(
                pltpu.make_async_copy(
                    src.at[pl.ds(i * half, half), :],
                    ref.at[:, pl.ds(LANES + k * width, width)],
                    sems.at[i, k],
                )
            )
    for copy in copies:
        copy.start()
    lane = lax.broadcasted_iota(jnp.int32, (tok_rows, LANES), 1)
    routes, weights = routes_ref[...].T, weights_ref[...].astype(jnp.float32).T
    dense = jnp.zeros((tok_rows, LANES), jnp.float32)
    for k in range(routes.shape[1]):
        dense += jnp.where(lane == routes[:, k : k + 1], weights[:, k : k + 1], 0.0)
    dense = dense.astype(jnp.bfloat16)
    low_ref[:, :LANES] = dense[:half]
    high_ref[:, :LANES] = dense[half:]
    for copy in copies:
        copy.wait()


def pack_call(routes_t, weights_t, x, y):
    tok_rows, width = x.shape
    out = pltpu.VMEM((tok_rows // 2, LANES + 2 * width), jnp.bfloat16)
    return pl.pallas_call(
        pack_kernel,
        out_shape=(out, out),
        in_specs=[VMEM_WHOLE] * 2 + [HBM_WHOLE] * 2,
        out_specs=(VMEM_WHOLE,) * 2,
        scratch_shapes=[pltpu.SemaphoreType.DMA((2, 2))],
        compiler_params=pltpu.CompilerParams(vmem_limit_bytes=4 * 2**20),
        name="pack_tokens",
    )(routes_t, weights_t, *away((x, y)))


def final_kernel(groups, routes_ref, *refs):
    sums, (token_ref, route_ref) = refs[:groups], refs[groups:]
    total = sums[0][...].astype(jnp.float32)
    for ref in sums[1:]:
        total = total + ref[...].astype(jnp.float32)
    width = token_ref.shape[1]
    token_ref[...] = total[:, :width].astype(jnp.bfloat16)
    scores, routes = total[:, width:].T, routes_ref[...]
    row = lax.broadcasted_iota(jnp.int32, scores.shape, 0)
    for k in range(routes.shape[0]):
        chosen = jnp.where(row == routes[k : k + 1, :], scores, 0.0)
        route_ref[k : k + 1, :] = jnp.sum(chosen, axis=0, keepdims=True)


def final_call(routes_t, sums):
    tok_rows, cols = sums[0].shape
    return pl.pallas_call(
        functools.partial(final_kernel, len(sums)),
        out_shape=(
            jax.ShapeDtypeStruct((tok_rows, cols - LANES), jnp.bfloat16),
            jax.ShapeDtypeStruct(routes_t.shape, jnp.float32),
        ),
        in_specs=[VMEM_WHOLE] * (1 + len(sums)),
        out_specs=(VMEM_WHOLE,) * 2,
        compiler_params=pltpu.CompilerParams(vmem_limit_bytes=4 * 2**20),
        name="token_sum",
    )(routes_t, *near(sums))


def after(value, *deps):
    return lax.optimization_barrier((value, *deps))[0]


def dense_body(
    tokens,
    cotangent,
    route_weights,
    routes,
    grid_gate,
    latent_gate,
    scale_gate,
    grid_up,
    latent_up,
    scale_up,
    grid_down,
    latent_down,
    scale_down,
):
    n_ep = lax.axis_size("ep")
    width = tokens.shape[1]
    where = jnp.stack([lax.axis_index("ep"), lax.axis_index("tp")]).astype(jnp.int32)
    hops = list(range(0, n_ep, 4))
    count = len(hops)
    halves = pack_call(routes.T, route_weights.T, tokens, cotangent)
    blocks = [halves]
    for g in range(1, count):
        held = (lambda piece: after(piece, blocks[-1][0])) if g == count - 1 and g > 1 else (lambda piece: piece)
        blocks.append([swap(held(piece), hops[g]) for piece in halves])
    parts = {}
    done, sums, planes = [], [], []

    def gather(g):
        low, high = blocks[g]
        low_x, high_y = swap(low, 2), swap(high, 0, 1)
        low_y, low_xy = swap(low, 0, 1), swap(low_x, 0, 1)
        high_x, high_xy = swap(high, 2), swap(high_y, 2)
        own = [low, low_x, low_y, low_xy, high, high_y, high_x, high_xy]
        parts[g] = own + [swap(piece, 1) for piece in own]

    mine = lax.axis_index("tp")
    width_of = width

    def relative(value, y_bit):
        return lax.dynamic_slice_in_dim(value, (mine ^ y_bit) * width_of, width_of, axis=-1)

    def weights_of(soften, grid, latent, scale, columns_scaled):
        return [
            soften(
                relative(grid, y_bit), relative(latent, y_bit), relative(scale, y_bit) if columns_scaled else scale
            ).astype(jnp.bfloat16)
            for y_bit in range(2)
        ]

    gather(0)
    weights = weights_of(soften_rows, grid_gate[0], latent_gate[0], scale_gate[0], False)
    held = parts[0][1]
    late_up, late_down = after(scale_up, held), after(scale_down, held)
    weights += weights_of(soften_rows, grid_up[0], latent_up[0], late_up[0], False)
    weights += weights_of(soften_cols, grid_down[0], latent_down[0], late_down[0], True)
    for g in range(1, count):
        gather(g)
    weight_sums = None
    for g in range(count):
        done.append(group_call(where, parts[g], weights))
        swapped = swap(done[g][1], 1)
        sums.append(core_call(done[g][0], swapped))
        own, to_y, to_x, to_far = sums[g]
        got = (swap(to_y, 0, 1), swap(to_x, 2), swap(to_far, 2, 1))
        planes.append(plane_call(own, *got, jnp.bfloat16 if g else jnp.float32))
        weight_sums = weight_sums_call(done[g][2], done[g][3], parts[g], weight_sums)
    arrived = [planes[0]]
    for g in range(1, count):
        arrived.append(swap(planes[g], hops[g]))
    token_grad, route_grad = final_call(routes.T, arrived)
    grads = grads_call(
        where,
        weight_sums,
        (latent_gate[0], latent_up[0], latent_down[0]),
        (scale_gate[0][:, None], scale_up[0][:, None], scale_down),
    )
    return (*(grad[None] for grad in grads), token_grad, route_grad.T)


def dense_fits(mesh, routes, weight):
    n_ep, n_tp = mesh.shape["ep"], mesh.shape["tp"]
    experts = weight.shape[0]
    fits = n_tp == 2 and n_ep % 8 == 0 and (n_ep & (n_ep - 1)) == 0
    return fits and experts == n_ep and experts <= LANES and 2 * routes.shape[1] >= experts


def solution(mesh):
    specs = dict(
        mesh=mesh,
        in_specs=(
            P("ep", "tp"),
            P("ep", "tp"),
            P("ep", None),
            P("ep", None),
            P("ep", "tp", None),
            P("ep", "tp", None),
            P("ep", "tp"),
            P("ep", "tp", None),
            P("ep", "tp", None),
            P("ep", "tp"),
            P("ep", "tp", None),
            P("ep", "tp", None),
            P("ep", None),
        ),
        out_specs=(
            P("ep", "tp", None),
            P("ep", "tp", None),
            P("ep", "tp", None),
            P("ep", "tp"),
            P("ep", None),
        ),
        check_vma=False,
    )
    dense = jax.shard_map(dense_body, **specs)
    routed = jax.shard_map(routed_body, **specs)

    def program(*args):
        if not dense_fits(mesh, args[3], args[4]):
            return routed(*args)
        return dense(*args)

    return program
```

```python
import functools

import jax
import jax.numpy as jnp
from jax import lax
from jax.experimental import pallas as pl
from jax.experimental.pallas import tpu as pltpu
from jax.sharding import PartitionSpec as P


temper = 0.25
grad_factor = 8.0


def soften_rows(grid, latent, scale):
    level = grid.astype(jnp.float32) + 0.5 * (1.0 + jnp.tanh(latent.astype(jnp.float32) / temper))
    return level * scale[:, None]


def soften_cols(grid, latent, scale):
    level = grid.astype(jnp.float32) + 0.5 * (1.0 + jnp.tanh(latent.astype(jnp.float32) / temper))
    return level * scale[None, :]


def latent_rows(grad_weight, latent, scale):
    slope = jnp.tanh(latent.astype(jnp.float32) / temper)
    return grad_factor * grad_weight * scale[:, None] * (1.0 - slope * slope) / (2.0 * temper)


def latent_cols(grad_weight, latent, scale):
    slope = jnp.tanh(latent.astype(jnp.float32) / temper)
    return grad_factor * grad_weight * scale[None, :] * (1.0 - slope * slope) / (2.0 * temper)


def block_slots(block_routes, experts, capacity):
    flat = block_routes.reshape(-1)
    columns = jnp.arange(experts, dtype=jnp.int32)
    onehot = (flat[:, None] == columns[None, :]).astype(jnp.int32)
    earlier = jnp.cumsum(onehot, axis=0) - onehot
    return flat * capacity + jnp.sum(earlier * onehot, axis=1)


def expert_backward(rows_x, rows_y, rows_p, w_gate, w_up, w_down):
    rowwise = (((1,), (1,)), ((), ()))
    gate = lax.dot_general(rows_x, w_gate, rowwise, preferred_element_type=jnp.float32)
    upper = lax.dot_general(rows_x, w_up, rowwise, preferred_element_type=jnp.float32)
    sigma = jax.nn.sigmoid(gate)
    active = gate * sigma
    hidden = active * upper
    weight = rows_p.astype(jnp.float32)[:, None]
    scaled = (hidden * weight).astype(jnp.bfloat16)
    back_hidden = lax.dot_general(rows_y, w_down, rowwise, preferred_element_type=jnp.float32)
    score = jnp.sum(hidden * back_hidden, axis=1)
    delta = back_hidden * weight
    grad_gate = (delta * upper * sigma * (1.0 + gate * (1.0 - sigma))).astype(jnp.bfloat16)
    grad_upper = (delta * active).astype(jnp.bfloat16)
    contract = (((0,), (0,)), ((), ()))
    grad_wg = lax.dot_general(grad_gate, rows_x, contract, preferred_element_type=jnp.float32)
    grad_wu = lax.dot_general(grad_upper, rows_x, contract, preferred_element_type=jnp.float32)
    grad_wd = lax.dot_general(scaled, rows_y, contract, preferred_element_type=jnp.float32)
    back_rows = jnp.dot(grad_gate, w_gate, preferred_element_type=jnp.float32)
    back_rows = back_rows + jnp.dot(grad_upper, w_up, preferred_element_type=jnp.float32)
    return (grad_wg, grad_wu, grad_wd, back_rows, score)


def pad_rows(values):
    return jnp.concatenate([values, jnp.zeros((1, values.shape[1]), values.dtype)], axis=0)


def routed_body(
    tokens,
    cotangent,
    route_weights,
    routes,
    grid_gate,
    latent_gate,
    scale_gate,
    grid_up,
    latent_up,
    scale_up,
    grid_down,
    latent_down,
    scale_down,
):
    n_ep = lax.axis_size("ep")
    experts = n_ep * grid_gate.shape[0]
    tok_rows, top = routes.shape
    capacity = min(tok_rows, 3 * tok_rows * top // (2 * experts))
    entries = tok_rows * top
    dest = block_slots(routes, experts, capacity)
    table = (
        jnp.full((experts * capacity,), entries, jnp.int32)
        .at[dest]
        .set(jnp.arange(entries, dtype=jnp.int32))
    )
    token_table = table // top
    weights_pad = jnp.concatenate(
        [route_weights.reshape(-1), jnp.zeros((1,), jnp.bfloat16)], axis=0
    )
    send_weights = weights_pad[table].reshape(experts, capacity)
    w_gate = soften_rows(grid_gate[0], latent_gate[0], scale_gate[0]).astype(jnp.bfloat16)
    w_up = soften_rows(grid_up[0], latent_up[0], scale_up[0]).astype(jnp.bfloat16)
    w_down = soften_cols(grid_down[0], latent_down[0], scale_down[0]).astype(jnp.bfloat16)
    part_x = pad_rows(tokens)[token_table].reshape(experts, capacity, -1)
    part_y = pad_rows(cotangent)[token_table].reshape(experts, capacity, -1)
    some_x, some_y, got_p = (
        lax.all_to_all(part_x, "ep", split_axis=0, concat_axis=0, tiled=True),
        lax.all_to_all(part_y, "ep", split_axis=0, concat_axis=0, tiled=True),
        lax.all_to_all(send_weights, "ep", split_axis=0, concat_axis=0, tiled=True),
    )
    got_x, got_y = (
        lax.all_gather(some_x, "tp", axis=2, tiled=True),
        lax.all_gather(some_y, "tp", axis=2, tiled=True),
    )
    width = got_x.shape[2]
    rows_x = got_x.reshape(-1, width)
    rows_y = got_y.reshape(-1, width)
    rows_p = got_p.reshape(-1)
    grad_wg, grad_wu, grad_wd, back_rows, score = expert_backward(
        rows_x, rows_y, rows_p, w_gate, w_up, w_down
    )
    grad_gate = latent_rows(grad_wg, latent_gate[0], scale_gate[0])[None]
    grad_upper = latent_rows(grad_wu, latent_up[0], scale_up[0])[None]
    grad_lower = latent_cols(grad_wd, latent_down[0], scale_down[0])[None]
    score = lax.psum(score.reshape(n_ep, capacity), "tp")
    back_rows = back_rows.reshape(n_ep, capacity, width)
    came_rows, came_score = (
        lax.all_to_all(back_rows, "ep", split_axis=0, concat_axis=0, tiled=True),
        lax.all_to_all(score, "ep", split_axis=0, concat_axis=0, tiled=True),
    )
    flat_rows = came_rows.reshape(experts * capacity, width)
    summed = jnp.sum(flat_rows[dest].reshape(tok_rows, top, width), axis=1)
    token_grad = lax.psum_scatter(summed, "tp", scatter_dimension=1, tiled=True).astype(
        jnp.bfloat16
    )
    route_grad = came_score.reshape(-1)[dest].reshape(tok_rows, top)
    return (grad_gate, grad_upper, grad_lower, token_grad, route_grad)


LANES = 128


def swap(value, ep_bits, tp_bits=0):
    n_ep, n_tp = lax.axis_size("ep"), lax.axis_size("tp")
    pairs = [
        (e * n_tp + t, (e ^ ep_bits) * n_tp + (t ^ tp_bits))
        for e in range(n_ep)
        for t in range(n_tp)
    ]
    return lax.ppermute(value, ("ep", "tp"), pairs)


PIECES = (
    (0, 0, 0),
    (1, 0, 0),
    (0, 1, 0),
    (1, 1, 0),
    (0, 0, 1),
    (0, 1, 1),
    (1, 0, 1),
    (1, 1, 1),
)


def stacked(pieces, y_bit, cols):
    parts = []
    for core in range(2):
        for x_bit in range(2):
            for upper in range(2):
                number = core * len(PIECES) + PIECES.index((x_bit, y_bit, upper))
                parts.append(pieces[number][:, cols])
    return parts


def nt(lhs, rhs):
    return lax.dot_general(lhs, rhs, (((1,), (1,)), ((), ())), preferred_element_type=jnp.float32)


def group_kernel(tok_rows, width, where_ref, *refs):
    pieces, weights = refs[:16], refs[16:22]
    outs, (deltas_ref, hid_ref) = refs[22:24], refs[24:26]
    both_s, back_s, weight_s = refs[26:]
    expert = where_ref[0]
    hid = hid_ref.shape[1]
    x_cols, y_cols = pl.ds(LANES, width), pl.ds(LANES + width, width)

    def whole(cols):
        halves = [jnp.concatenate(stacked(pieces, y_bit, cols), axis=0) for y_bit in range(2)]
        return jnp.concatenate(halves, axis=1)

    def weight_rows(i):
        return jnp.concatenate([weights[2 * i][...], weights[2 * i + 1][...]], axis=1)

    both_s[...] = nt(whole(x_cols), jnp.concatenate([weight_rows(0), weight_rows(1)], axis=0))
    back_s[...] = nt(whole(y_cols), weight_rows(2))
    part = tok_rows // 2
    for i, dense in enumerate(stacked(pieces, 0, pl.ds(0, LANES))):
        lane = lax.broadcasted_iota(jnp.int32, dense.shape, 1)
        weight_s[i * part : (i + 1) * part] = jnp.sum(
            jnp.where(lane == expert, dense.astype(jnp.float32), 0.0), axis=1, keepdims=True
        )
    chunk = tok_rows // 4
    for i in range(both_s.shape[0] // chunk):
        rows = pl.ds(i * chunk, chunk)
        gate, upper, back = both_s[rows, :hid], both_s[rows, hid:], back_s[rows, :]
        weight = weight_s[rows]
        sigma = jax.nn.sigmoid(gate)
        active = gate * sigma
        hidden = active * upper
        score = jnp.sum(hidden * back, axis=1, keepdims=True)
        delta = back * weight
        deltas_ref[rows, :hid] = (
            delta * upper * sigma * (1.0 + gate * (1.0 - sigma))
        ).astype(jnp.bfloat16)
        deltas_ref[rows, hid:] = (delta * active).astype(jnp.bfloat16)
        hid_ref[rows, :] = (hidden * weight).astype(jnp.bfloat16)
        lane = lax.broadcasted_iota(jnp.int32, (chunk, LANES), 1)
        spread = jnp.where(lane == expert, score, 0.0).astype(jnp.bfloat16)
        block, row = divmod(i * chunk, tok_rows)
        core, x_bit = divmod(block, 2)
        for y_bit in range(2):
            outs[core][y_bit, x_bit, pl.ds(row, chunk), pl.ds(width, LANES)] = spread
    for y_bit in range(2):
        both = jnp.concatenate([weights[y_bit][...], weights[2 + y_bit][...]], axis=0)
        rows_back = jnp.dot(deltas_ref[...], both, preferred_element_type=jnp.float32)
        rows_back = rows_back.astype(jnp.bfloat16)
        for block in range(4):
            core, x_bit = divmod(block, 2)
            outs[core][y_bit, x_bit, :, pl.ds(0, width)] = rows_back[
                block * tok_rows : (block + 1) * tok_rows
            ]


VMEM_WHOLE = pl.BlockSpec(memory_space=pltpu.VMEM)
SMEM_WHOLE = pl.BlockSpec(memory_space=pltpu.SMEM)
HBM_WHOLE = pl.BlockSpec(memory_space=pltpu.HBM)


def away(values):
    return [pltpu.with_memory_space_constraint(value, pltpu.HBM) for value in values]


def near(values):
    return [pltpu.with_memory_space_constraint(value, pltpu.VMEM) for value in values]


def group_call(where, pieces, weights):
    tok_rows = 2 * pieces[0].shape[0]
    hid, width = weights[0].shape
    rows = 4 * tok_rows
    out = pltpu.VMEM((2, 2, tok_rows, width + LANES), jnp.bfloat16)
    return pl.pallas_call(
        functools.partial(group_kernel, tok_rows, width),
        out_shape=(
            out,
            out,
            pltpu.VMEM((rows, 2 * hid), jnp.bfloat16),
            pltpu.VMEM((rows, hid), jnp.bfloat16),
        ),
        in_specs=[SMEM_WHOLE] + [VMEM_WHOLE] * 22,
        out_specs=(VMEM_WHOLE,) * 4,
        scratch_shapes=[
            pltpu.VMEM((rows, 2 * hid), jnp.float32),
            pltpu.VMEM((rows, hid), jnp.float32),
            pltpu.VMEM((rows, 1), jnp.float32),
        ],
        cost_estimate=pl.CostEstimate(
            flops=20 * rows * hid * width, transcendentals=rows * hid, bytes_accessed=2 * 4 * rows * width * 2
        ),
        compiler_params=pltpu.CompilerParams(vmem_limit_bytes=6 * 2**20),
        name="expert_rows",
    )(where, *near(pieces), *near(weights))


def core_kernel(keep_ref, got_ref, own_ref, y_ref, x_ref, far_ref):
    for (y_bit, x_bit), ref in (((1, 0), y_ref), ((0, 1), x_ref), ((1, 1), far_ref), ((0, 0), own_ref)):
        total = keep_ref[y_bit, x_bit].astype(jnp.float32) + got_ref[y_bit, x_bit].astype(jnp.float32)
        ref[...] = total.astype(ref.dtype)


def core_call(keep, got):
    shape = keep.shape[2:]
    sent = pltpu.VMEM(shape, jnp.bfloat16)
    return pl.pallas_call(
        core_kernel,
        out_shape=(pltpu.VMEM(shape, jnp.float32), sent, sent, sent),
        in_specs=[VMEM_WHOLE] * 2,
        out_specs=(VMEM_WHOLE,) * 4,
        compiler_params=pltpu.CompilerParams(vmem_limit_bytes=4 * 2**20),
        name="core_sum",
    )(*near((keep, got)))


def plane_kernel(own_ref, y_ref, x_ref, far_ref, out_ref):
    total = own_ref[...] + y_ref[...].astype(jnp.float32)
    total = total + x_ref[...].astype(jnp.float32) + far_ref[...].astype(jnp.float32)
    out_ref[...] = total.astype(out_ref.dtype)


def plane_call(own, from_y, from_x, from_far, dtype):
    return pl.pallas_call(
        plane_kernel,
        out_shape=pltpu.VMEM(own.shape, dtype),
        in_specs=[VMEM_WHOLE] * 4,
        out_specs=VMEM_WHOLE,
        compiler_params=pltpu.CompilerParams(vmem_limit_bytes=4 * 2**20),
        name="plane_sum",
    )(*near((own, from_y, from_x, from_far)))


def weight_sums_kernel(first, width, *refs):
    deltas_ref, hid_ref, pieces = refs[0], refs[1], refs[2:18]
    sums = refs[18:20] if first else refs[20:22]
    flipped = refs[-1]
    count = deltas_ref.shape[1]
    flipped[:count] = deltas_ref[...].T
    flipped[count:] = hid_ref[...].T
    tile = width // 2
    for rows, start, out in (
        (pl.ds(0, count), LANES, sums[0]),
        (pl.ds(count, hid_ref.shape[1]), LANES + width, sums[1]),
    ):
        for y_bit in range(2):
            for t in range(2):
                data = jnp.concatenate(stacked(pieces, y_bit, pl.ds(start + t * tile, tile)), axis=0)
                part = jnp.dot(flipped[rows], data, preferred_element_type=jnp.float32)
                here = pl.ds(y_bit * width + t * tile, tile)
                out[:, here] = part if first else out[:, here] + part


def weight_sums_call(deltas, hidden, pieces, sums):
    rows, count = deltas.shape
    hid, width = hidden.shape[1], (pieces[0].shape[1] - LANES) // 2
    first = sums is None
    outs = (pltpu.VMEM((count, 2 * width), jnp.float32), pltpu.VMEM((hid, 2 * width), jnp.float32))
    held = () if first else tuple(near(sums))
    return pl.pallas_call(
        functools.partial(weight_sums_kernel, first, width),
        out_shape=outs,
        in_specs=[VMEM_WHOLE] * (18 + len(held)),
        out_specs=(VMEM_WHOLE,) * 2,
        scratch_shapes=[pltpu.VMEM((count + hid, rows), jnp.bfloat16)],
        input_output_aliases={} if first else {18: 0, 19: 1},
        compiler_params=pltpu.CompilerParams(vmem_limit_bytes=8 * 2**20),
        cost_estimate=pl.CostEstimate(
            flops=4 * (count + hid) * rows * width, transcendentals=0, bytes_accessed=4 * rows * width * 2
        ),
        name="weight_sums",
    )(*near((deltas, hidden)), *near(pieces), *held)


def column(row):
    return jnp.broadcast_to(row, (8, row.shape[1])).T[:, :1]


def soften_kernel(by_column, where_ref, *refs):
    count = len(by_column)
    grids, latents, scales = refs[:count], refs[count : 2 * count], refs[2 * count : 3 * count]
    outs = refs[3 * count : 5 * count]
    held, sems = refs[5 * count :]
    mine = where_ref[1]
    width = outs[0].shape[1]
    loads = []
    for i in range(count):
        for y_bit in range(2):
            there = pl.ds(pl.multiple_of(jnp.bitwise_xor(mine, y_bit) * width, LANES), width)
            for k, src in enumerate((grids[i], latents[i])):
                loads.append(
                    pltpu.make_async_copy(src.at[:, there], held.at[i, y_bit, k], sems.at[i, y_bit, k])
                )
    for copy in loads:
        copy.start()
    for i in range(count):
        for y_bit in range(2):
            for copy in loads[4 * i + 2 * y_bit : 4 * i + 2 * y_bit + 2]:
                copy.wait()
            there = pl.ds(pl.multiple_of(jnp.bitwise_xor(mine, y_bit) * width, LANES), width)
            scale = scales[i][:, there] if by_column[i] else column(scales[i][...])
            soft = 0.5 * (1.0 + jnp.tanh(held[i, y_bit, 1].astype(jnp.float32) / temper))
            level = held[i, y_bit, 0].astype(jnp.float32) + soft
            outs[2 * i + y_bit][...] = (level * scale).astype(jnp.bfloat16)


def soften_call(where, grids, latents, scales, by_column):
    count = len(grids)
    hid, feat = grids[0].shape
    out = pltpu.VMEM((hid, feat // 2), jnp.bfloat16)
    return pl.pallas_call(
        functools.partial(soften_kernel, by_column),
        out_shape=(out,) * (2 * count),
        in_specs=[SMEM_WHOLE] + [HBM_WHOLE] * (2 * count) + [VMEM_WHOLE] * count,
        out_specs=(VMEM_WHOLE,) * (2 * count),
        scratch_shapes=[
            pltpu.VMEM((count, 2, 2, hid, feat // 2), jnp.bfloat16),
            pltpu.SemaphoreType.DMA((count, 2, 2)),
        ],
        compiler_params=pltpu.CompilerParams(vmem_limit_bytes=12 * 2**20),
        cost_estimate=pl.CostEstimate(
            flops=5 * count * hid * feat,
            transcendentals=count * hid * feat,
            bytes_accessed=count * hid * feat * 6,
        ),
        name="soften",
    )(where, *away(grids), *away(latents), *scales)


def grads_kernel(where_ref, *refs):
    sums, latents, scales, outs = refs[0:2], refs[2:5], refs[5:8], refs[8:11]
    lats, stage, lsems, osems = refs[11:]
    mine = where_ref[1]
    slots = stage.shape[0]
    hid, feat = latents[0].shape
    width, tile = feat // 2, stage.shape[2]
    lat_copies = [pltpu.make_async_copy(latents[i], lats.at[i], lsems.at[i]) for i in range(3)]
    for copy in lat_copies:
        copy.start()
    writes = []
    row_scales = [column(scales[i][...]) for i in range(2)]
    for i in range(3):
        lat_copies[i].wait()
        for y_bit in range(2):
            for t in range(width // tile):
                there = jnp.bitwise_xor(mine, y_bit) * width + t * tile
                there = pl.ds(pl.multiple_of(there, LANES), tile)
                here = pl.ds(y_bit * width + t * tile, tile)
                slope = jnp.tanh(lats[i, :, there].astype(jnp.float32) / temper)
                scale = scales[i][:, there] if i == 2 else row_scales[i]
                factor = (grad_factor / (2.0 * temper)) * scale * (1.0 - slope * slope)
                total = sums[1][:, here] if i == 2 else sums[0][pl.ds(i * hid, hid), here]
                slot = len(writes) % slots
                if len(writes) >= slots:
                    writes[len(writes) - slots].wait()
                stage[slot] = total * factor
                copy = pltpu.make_async_copy(stage.at[slot], outs[i].at[:, there], osems.at[slot])
                copy.start()
                writes.append(copy)
    for copy in writes[-slots:]:
        copy.wait()


def grads_call(where, sums, latents, scales):
    hid, feat = latents[0].shape
    out = jax.ShapeDtypeStruct((hid, feat), jnp.float32)
    return pl.pallas_call(
        grads_kernel,
        out_shape=(out,) * 3,
        in_specs=[SMEM_WHOLE] + [VMEM_WHOLE] * 2 + [HBM_WHOLE] * 3 + [VMEM_WHOLE] * 3,
        out_specs=(HBM_WHOLE,) * 3,
        scratch_shapes=[
            pltpu.VMEM((3, hid, feat), jnp.bfloat16),
            pltpu.VMEM((6, hid, feat // 4), jnp.float32),
            pltpu.SemaphoreType.DMA((3,)),
            pltpu.SemaphoreType.DMA((6,)),
        ],
        compiler_params=pltpu.CompilerParams(vmem_limit_bytes=12 * 2**20),
        cost_estimate=pl.CostEstimate(
            flops=18 * hid * feat,
            transcendentals=3 * hid * feat,
            bytes_accessed=3 * hid * feat * 6,
        ),
        name="latent_grads",
    )(where, *near(sums), *away(latents), *scales)


def pack_kernel(
    routes_hbm, weights_hbm, x_hbm, y_hbm, low_ref, high_ref, routes_ref, weights_ref, sems, small_sems
):
    tok_rows, width = x_hbm.shape
    half = tok_rows // 2
    small = [
        pltpu.make_async_copy(routes_hbm, routes_ref, small_sems.at[0]),
        pltpu.make_async_copy(weights_hbm, weights_ref, small_sems.at[1]),
    ]
    for copy in small:
        copy.start()
    copies = []
    for i, ref in enumerate((low_ref, high_ref)):
        for k, src in enumerate((x_hbm, y_hbm)):
            copies.append(
                pltpu.make_async_copy(
                    src.at[pl.ds(i * half, half), :],
                    ref.at[:, pl.ds(LANES + k * width, width)],
                    sems.at[i, k],
                )
            )
    for copy in copies:
        copy.start()
    for copy in small:
        copy.wait()
    lane = lax.broadcasted_iota(jnp.int32, (tok_rows, LANES), 1)
    routes, weights = routes_ref[...].T, weights_ref[...].astype(jnp.float32).T
    dense = jnp.zeros((tok_rows, LANES), jnp.float32)
    for k in range(routes.shape[1]):
        dense += jnp.where(lane == routes[:, k : k + 1], weights[:, k : k + 1], 0.0)
    dense = dense.astype(jnp.bfloat16)
    low_ref[:, :LANES] = dense[:half]
    high_ref[:, :LANES] = dense[half:]
    for copy in copies:
        copy.wait()


def pack_call(routes_t, weights_t, x, y):
    tok_rows, width = x.shape
    out = pltpu.VMEM((tok_rows // 2, LANES + 2 * width), jnp.bfloat16)
    return pl.pallas_call(
        pack_kernel,
        out_shape=(out, out),
        in_specs=[HBM_WHOLE] * 4,
        out_specs=(VMEM_WHOLE,) * 2,
        scratch_shapes=[
            pltpu.VMEM(routes_t.shape, routes_t.dtype),
            pltpu.VMEM(weights_t.shape, weights_t.dtype),
            pltpu.SemaphoreType.DMA((2, 2)),
            pltpu.SemaphoreType.DMA((2,)),
        ],
        compiler_params=pltpu.CompilerParams(vmem_limit_bytes=4 * 2**20),
        name="pack_tokens",
    )(*away((routes_t, weights_t, x, y)))


def final_kernel(groups, routes_ref, *refs):
    sums, (token_ref, route_ref) = refs[:groups], refs[groups:]
    total = sums[0][...].astype(jnp.float32)
    for ref in sums[1:]:
        total = total + ref[...].astype(jnp.float32)
    width = token_ref.shape[1]
    token_ref[...] = total[:, :width].astype(jnp.bfloat16)
    scores, routes = total[:, width:].T, routes_ref[...]
    row = lax.broadcasted_iota(jnp.int32, scores.shape, 0)
    for k in range(routes.shape[0]):
        chosen = jnp.where(row == routes[k : k + 1, :], scores, 0.0)
        route_ref[k : k + 1, :] = jnp.sum(chosen, axis=0, keepdims=True)


def final_call(routes_t, sums):
    tok_rows, cols = sums[0].shape
    return pl.pallas_call(
        functools.partial(final_kernel, len(sums)),
        out_shape=(
            jax.ShapeDtypeStruct((tok_rows, cols - LANES), jnp.bfloat16),
            jax.ShapeDtypeStruct(routes_t.shape, jnp.float32),
        ),
        in_specs=[VMEM_WHOLE] * (1 + len(sums)),
        out_specs=(VMEM_WHOLE,) * 2,
        compiler_params=pltpu.CompilerParams(vmem_limit_bytes=4 * 2**20),
        name="token_sum",
    )(routes_t, *near(sums))


def after(value, *deps):
    return lax.optimization_barrier((value, *deps))[0]


def dense_body(
    tokens,
    cotangent,
    route_weights,
    routes,
    grid_gate,
    latent_gate,
    scale_gate,
    grid_up,
    latent_up,
    scale_up,
    grid_down,
    latent_down,
    scale_down,
):
    n_ep = lax.axis_size("ep")
    where = jnp.stack([lax.axis_index("ep"), lax.axis_index("tp")]).astype(jnp.int32)
    hops = list(range(0, n_ep, 4))
    count = len(hops)
    halves = pack_call(routes.T, route_weights.T, tokens, cotangent)
    blocks = [halves]
    for g in range(1, count):
        held = (lambda piece: after(piece, blocks[-1][0])) if g == count - 1 and g > 1 else (lambda piece: piece)
        blocks.append([swap(held(piece), hops[g]) for piece in halves])
    parts = {}
    done, sums, planes = [], [], []

    def gather(g):
        low, high = blocks[g]
        low_x, high_y = swap(low, 2), swap(high, 0, 1)
        low_y, low_xy = swap(low, 0, 1), swap(low_x, 0, 1)
        high_x, high_xy = swap(high, 2), swap(high_y, 2)
        own = [low, low_x, low_y, low_xy, high, high_y, high_x, high_xy]
        parts[g] = own + [swap(piece, 1) for piece in own]

    gather(0)
    weights = list(soften_call(where, (grid_gate[0],), (latent_gate[0],), (scale_gate,), (False,)))
    late = after(where, parts[0][1])
    weights += soften_call(
        late,
        (grid_up[0], grid_down[0]),
        (latent_up[0], latent_down[0]),
        (scale_up, scale_down),
        (False, True),
    )
    for g in range(1, count):
        gather(g)
    weight_sums = None
    for g in range(count):
        done.append(group_call(where, parts[g], weights))
        swapped = swap(done[g][1], 1)
        sums.append(core_call(done[g][0], swapped))
        own, to_y, to_x, to_far = sums[g]
        got = (swap(to_y, 0, 1), swap(to_x, 2), swap(to_far, 2, 1))
        planes.append(plane_call(own, *got, jnp.bfloat16 if g else jnp.float32))
        weight_sums = weight_sums_call(done[g][2], done[g][3], parts[g], weight_sums)
    arrived = [planes[0]]
    for g in range(1, count):
        arrived.append(swap(planes[g], hops[g]))
    token_grad, route_grad = final_call(routes.T, arrived)
    grads = grads_call(
        where,
        weight_sums,
        (latent_gate[0], latent_up[0], latent_down[0]),
        (scale_gate, scale_up, scale_down),
    )
    return (*(grad[None] for grad in grads), token_grad, route_grad.T)


def dense_fits(mesh, routes, weight):
    n_ep, n_tp = mesh.shape["ep"], mesh.shape["tp"]
    experts = weight.shape[0]
    fits = n_tp == 2 and n_ep % 8 == 0 and (n_ep & (n_ep - 1)) == 0
    return fits and experts == n_ep and experts <= LANES and 2 * routes.shape[1] >= experts


def solution(mesh):
    specs = dict(
        mesh=mesh,
        in_specs=(
            P("ep", "tp"),
            P("ep", "tp"),
            P("ep", None),
            P("ep", None),
            P("ep", "tp", None),
            P("ep", "tp", None),
            P("ep", "tp"),
            P("ep", "tp", None),
            P("ep", "tp", None),
            P("ep", "tp"),
            P("ep", "tp", None),
            P("ep", "tp", None),
            P("ep", None),
        ),
        out_specs=(
            P("ep", "tp", None),
            P("ep", "tp", None),
            P("ep", "tp", None),
            P("ep", "tp"),
            P("ep", None),
        ),
        check_vma=False,
    )
    dense = jax.shard_map(dense_body, **specs)
    routed = jax.shard_map(routed_body, **specs)

    def program(*args):
        if not dense_fits(mesh, args[3], args[4]):
            return routed(*args)
        return dense(*args)

    return program
```

```python
import functools

import jax
import jax.numpy as jnp
from jax import lax
from jax.experimental import pallas as pl
from jax.experimental.pallas import tpu as pltpu
from jax.sharding import PartitionSpec as P


temper = 0.25
grad_factor = 8.0


def soften_rows(grid, latent, scale):
    level = grid.astype(jnp.float32) + 0.5 * (1.0 + jnp.tanh(latent.astype(jnp.float32) / temper))
    return level * scale[:, None]


def soften_cols(grid, latent, scale):
    level = grid.astype(jnp.float32) + 0.5 * (1.0 + jnp.tanh(latent.astype(jnp.float32) / temper))
    return level * scale[None, :]


def latent_rows(grad_weight, latent, scale):
    slope = jnp.tanh(latent.astype(jnp.float32) / temper)
    return grad_factor * grad_weight * scale[:, None] * (1.0 - slope * slope) / (2.0 * temper)


def latent_cols(grad_weight, latent, scale):
    slope = jnp.tanh(latent.astype(jnp.float32) / temper)
    return grad_factor * grad_weight * scale[None, :] * (1.0 - slope * slope) / (2.0 * temper)


def block_slots(block_routes, experts, capacity):
    flat = block_routes.reshape(-1)
    columns = jnp.arange(experts, dtype=jnp.int32)
    onehot = (flat[:, None] == columns[None, :]).astype(jnp.int32)
    earlier = jnp.cumsum(onehot, axis=0) - onehot
    return flat * capacity + jnp.sum(earlier * onehot, axis=1)


def expert_backward(rows_x, rows_y, rows_p, w_gate, w_up, w_down):
    rowwise = (((1,), (1,)), ((), ()))
    gate = lax.dot_general(rows_x, w_gate, rowwise, preferred_element_type=jnp.float32)
    upper = lax.dot_general(rows_x, w_up, rowwise, preferred_element_type=jnp.float32)
    sigma = jax.nn.sigmoid(gate)
    active = gate * sigma
    hidden = active * upper
    weight = rows_p.astype(jnp.float32)[:, None]
    scaled = (hidden * weight).astype(jnp.bfloat16)
    back_hidden = lax.dot_general(rows_y, w_down, rowwise, preferred_element_type=jnp.float32)
    score = jnp.sum(hidden * back_hidden, axis=1)
    delta = back_hidden * weight
    grad_gate = (delta * upper * sigma * (1.0 + gate * (1.0 - sigma))).astype(jnp.bfloat16)
    grad_upper = (delta * active).astype(jnp.bfloat16)
    contract = (((0,), (0,)), ((), ()))
    grad_wg = lax.dot_general(grad_gate, rows_x, contract, preferred_element_type=jnp.float32)
    grad_wu = lax.dot_general(grad_upper, rows_x, contract, preferred_element_type=jnp.float32)
    grad_wd = lax.dot_general(scaled, rows_y, contract, preferred_element_type=jnp.float32)
    back_rows = jnp.dot(grad_gate, w_gate, preferred_element_type=jnp.float32)
    back_rows = back_rows + jnp.dot(grad_upper, w_up, preferred_element_type=jnp.float32)
    return (grad_wg, grad_wu, grad_wd, back_rows, score)


def pad_rows(values):
    return jnp.concatenate([values, jnp.zeros((1, values.shape[1]), values.dtype)], axis=0)


def routed_body(
    tokens,
    cotangent,
    route_weights,
    routes,
    grid_gate,
    latent_gate,
    scale_gate,
    grid_up,
    latent_up,
    scale_up,
    grid_down,
    latent_down,
    scale_down,
):
    n_ep = lax.axis_size("ep")
    experts = n_ep * grid_gate.shape[0]
    tok_rows, top = routes.shape
    capacity = min(tok_rows, 3 * tok_rows * top // (2 * experts))
    entries = tok_rows * top
    dest = block_slots(routes, experts, capacity)
    table = (
        jnp.full((experts * capacity,), entries, jnp.int32)
        .at[dest]
        .set(jnp.arange(entries, dtype=jnp.int32))
    )
    token_table = table // top
    weights_pad = jnp.concatenate(
        [route_weights.reshape(-1), jnp.zeros((1,), jnp.bfloat16)], axis=0
    )
    send_weights = weights_pad[table].reshape(experts, capacity)
    w_gate = soften_rows(grid_gate[0], latent_gate[0], scale_gate[0]).astype(jnp.bfloat16)
    w_up = soften_rows(grid_up[0], latent_up[0], scale_up[0]).astype(jnp.bfloat16)
    w_down = soften_cols(grid_down[0], latent_down[0], scale_down[0]).astype(jnp.bfloat16)
    part_x = pad_rows(tokens)[token_table].reshape(experts, capacity, -1)
    part_y = pad_rows(cotangent)[token_table].reshape(experts, capacity, -1)
    some_x, some_y, got_p = (
        lax.all_to_all(part_x, "ep", split_axis=0, concat_axis=0, tiled=True),
        lax.all_to_all(part_y, "ep", split_axis=0, concat_axis=0, tiled=True),
        lax.all_to_all(send_weights, "ep", split_axis=0, concat_axis=0, tiled=True),
    )
    got_x, got_y = (
        lax.all_gather(some_x, "tp", axis=2, tiled=True),
        lax.all_gather(some_y, "tp", axis=2, tiled=True),
    )
    width = got_x.shape[2]
    rows_x = got_x.reshape(-1, width)
    rows_y = got_y.reshape(-1, width)
    rows_p = got_p.reshape(-1)
    grad_wg, grad_wu, grad_wd, back_rows, score = expert_backward(
        rows_x, rows_y, rows_p, w_gate, w_up, w_down
    )
    grad_gate = latent_rows(grad_wg, latent_gate[0], scale_gate[0])[None]
    grad_upper = latent_rows(grad_wu, latent_up[0], scale_up[0])[None]
    grad_lower = latent_cols(grad_wd, latent_down[0], scale_down[0])[None]
    score = lax.psum(score.reshape(n_ep, capacity), "tp")
    back_rows = back_rows.reshape(n_ep, capacity, width)
    came_rows, came_score = (
        lax.all_to_all(back_rows, "ep", split_axis=0, concat_axis=0, tiled=True),
        lax.all_to_all(score, "ep", split_axis=0, concat_axis=0, tiled=True),
    )
    flat_rows = came_rows.reshape(experts * capacity, width)
    summed = jnp.sum(flat_rows[dest].reshape(tok_rows, top, width), axis=1)
    token_grad = lax.psum_scatter(summed, "tp", scatter_dimension=1, tiled=True).astype(
        jnp.bfloat16
    )
    route_grad = came_score.reshape(-1)[dest].reshape(tok_rows, top)
    return (grad_gate, grad_upper, grad_lower, token_grad, route_grad)


LANES = 128
STEP = 32


def swap(value, ep_bits, tp_bits=0):
    n_ep, n_tp = lax.axis_size("ep"), lax.axis_size("tp")
    pairs = [
        (e * n_tp + t, (e ^ ep_bits) * n_tp + (t ^ tp_bits))
        for e in range(n_ep)
        for t in range(n_tp)
    ]
    return lax.ppermute(value, ("ep", "tp"), pairs)


PIECES = (
    (0, 0, 0),
    (1, 0, 0),
    (0, 1, 0),
    (1, 1, 0),
    (0, 0, 1),
    (0, 1, 1),
    (1, 0, 1),
    (1, 1, 1),
)


def stacked(pieces, y_bit, cols):
    parts = []
    for core in range(2):
        for x_bit in range(2):
            for upper in range(2):
                number = core * len(PIECES) + PIECES.index((x_bit, y_bit, upper))
                parts.append(pieces[number][:, cols])
    return parts


def nt(lhs, rhs):
    return lax.dot_general(lhs, rhs, (((1,), (1,)), ((), ())), preferred_element_type=jnp.float32)


def group_kernel(tok_rows, width, where_ref, *refs):
    pieces, weights = refs[:16], refs[16:22]
    outs, (deltas_ref, hid_ref) = refs[22:24], refs[24:26]
    both_s, back_s, weight_s = refs[26:]
    expert = where_ref[0]
    hid = hid_ref.shape[1]
    x_cols, y_cols = pl.ds(LANES, width), pl.ds(LANES + width, width)

    def whole(cols):
        halves = [jnp.concatenate(stacked(pieces, y_bit, cols), axis=0) for y_bit in range(2)]
        return jnp.concatenate(halves, axis=1)

    def weight_rows(i):
        return jnp.concatenate([weights[2 * i][...], weights[2 * i + 1][...]], axis=1)

    both_s[...] = nt(whole(x_cols), jnp.concatenate([weight_rows(0), weight_rows(1)], axis=0))
    back_s[...] = nt(whole(y_cols), weight_rows(2))
    part = tok_rows // 2
    for i, dense in enumerate(stacked(pieces, 0, pl.ds(0, LANES))):
        lane = lax.broadcasted_iota(jnp.int32, dense.shape, 1)
        weight_s[i * part : (i + 1) * part] = jnp.sum(
            jnp.where(lane == expert, dense.astype(jnp.float32), 0.0), axis=1, keepdims=True
        )
    chunk = tok_rows // 4
    for i in range(both_s.shape[0] // chunk):
        rows = pl.ds(i * chunk, chunk)
        gate, upper, back = both_s[rows, :hid], both_s[rows, hid:], back_s[rows, :]
        weight = weight_s[rows]
        sigma = jax.nn.sigmoid(gate)
        active = gate * sigma
        hidden = active * upper
        score = jnp.sum(hidden * back, axis=1, keepdims=True)
        delta = back * weight
        deltas_ref[rows, :hid] = (
            delta * upper * sigma * (1.0 + gate * (1.0 - sigma))
        ).astype(jnp.bfloat16)
        deltas_ref[rows, hid:] = (delta * active).astype(jnp.bfloat16)
        hid_ref[rows, :] = (hidden * weight).astype(jnp.bfloat16)
        lane = lax.broadcasted_iota(jnp.int32, (chunk, LANES), 1)
        spread = jnp.where(lane == expert, score, 0.0).astype(jnp.bfloat16)
        block, row = divmod(i * chunk, tok_rows)
        core, x_bit = divmod(block, 2)
        for y_bit in range(2):
            outs[core][y_bit, x_bit, pl.ds(row, chunk), pl.ds(width, LANES)] = spread
    for y_bit in range(2):
        both = jnp.concatenate([weights[y_bit][...], weights[2 + y_bit][...]], axis=0)
        rows_back = jnp.dot(deltas_ref[...], both, preferred_element_type=jnp.float32)
        rows_back = rows_back.astype(jnp.bfloat16)
        for block in range(4):
            core, x_bit = divmod(block, 2)
            outs[core][y_bit, x_bit, :, pl.ds(0, width)] = rows_back[
                block * tok_rows : (block + 1) * tok_rows
            ]


VMEM_WHOLE = pl.BlockSpec(memory_space=pltpu.VMEM)
SMEM_WHOLE = pl.BlockSpec(memory_space=pltpu.SMEM)
HBM_WHOLE = pl.BlockSpec(memory_space=pltpu.HBM)


def away(values):
    return [pltpu.with_memory_space_constraint(value, pltpu.HBM) for value in values]


def near(values):
    return [pltpu.with_memory_space_constraint(value, pltpu.VMEM) for value in values]


def group_call(where, pieces, weights):
    tok_rows = 2 * pieces[0].shape[0]
    hid, width = weights[0].shape
    rows = 4 * tok_rows
    out = pltpu.VMEM((2, 2, tok_rows, width + LANES), jnp.bfloat16)
    return pl.pallas_call(
        functools.partial(group_kernel, tok_rows, width),
        out_shape=(
            out,
            out,
            pltpu.VMEM((rows, 2 * hid), jnp.bfloat16),
            pltpu.VMEM((rows, hid), jnp.bfloat16),
        ),
        in_specs=[SMEM_WHOLE] + [VMEM_WHOLE] * 22,
        out_specs=(VMEM_WHOLE,) * 4,
        scratch_shapes=[
            pltpu.VMEM((rows, 2 * hid), jnp.float32),
            pltpu.VMEM((rows, hid), jnp.float32),
            pltpu.VMEM((rows, 1), jnp.float32),
        ],
        cost_estimate=pl.CostEstimate(
            flops=20 * rows * hid * width, transcendentals=rows * hid, bytes_accessed=2 * 4 * rows * width * 2
        ),
        compiler_params=pltpu.CompilerParams(vmem_limit_bytes=6 * 2**20),
        name="expert_rows",
    )(where, *near(pieces), *near(weights))


def core_kernel(keep_ref, got_ref, own_ref, y_ref, x_ref, far_ref):
    for (y_bit, x_bit), ref in (((1, 0), y_ref), ((0, 1), x_ref), ((1, 1), far_ref), ((0, 0), own_ref)):
        total = keep_ref[y_bit, x_bit].astype(jnp.float32) + got_ref[y_bit, x_bit].astype(jnp.float32)
        ref[...] = total.astype(ref.dtype)


def core_call(keep, got):
    shape = keep.shape[2:]
    sent = pltpu.VMEM(shape, jnp.bfloat16)
    return pl.pallas_call(
        core_kernel,
        out_shape=(pltpu.VMEM(shape, jnp.float32), sent, sent, sent),
        in_specs=[VMEM_WHOLE] * 2,
        out_specs=(VMEM_WHOLE,) * 4,
        compiler_params=pltpu.CompilerParams(vmem_limit_bytes=4 * 2**20),
        name="core_sum",
    )(*near((keep, got)))


def plane_kernel(own_ref, y_ref, x_ref, far_ref, out_ref):
    total = own_ref[...] + y_ref[...].astype(jnp.float32)
    total = total + x_ref[...].astype(jnp.float32) + far_ref[...].astype(jnp.float32)
    out_ref[...] = total.astype(out_ref.dtype)


def plane_call(own, from_y, from_x, from_far, dtype):
    return pl.pallas_call(
        plane_kernel,
        out_shape=pltpu.VMEM(own.shape, dtype),
        in_specs=[VMEM_WHOLE] * 4,
        out_specs=VMEM_WHOLE,
        compiler_params=pltpu.CompilerParams(vmem_limit_bytes=4 * 2**20),
        name="plane_sum",
    )(*near((own, from_y, from_x, from_far)))


def weight_sums_kernel(first, width, *refs):
    deltas_ref, hid_ref, pieces = refs[0], refs[1], refs[2:18]
    sums = refs[18:20] if first else refs[20:22]
    flipped = refs[-1]
    count = deltas_ref.shape[1]
    flipped[:count] = deltas_ref[...].T
    flipped[count:] = hid_ref[...].T
    tile = width // 2
    for rows, start, out in (
        (pl.ds(0, count), LANES, sums[0]),
        (pl.ds(count, hid_ref.shape[1]), LANES + width, sums[1]),
    ):
        for y_bit in range(2):
            for t in range(2):
                data = jnp.concatenate(stacked(pieces, y_bit, pl.ds(start + t * tile, tile)), axis=0)
                part = jnp.dot(flipped[rows], data, preferred_element_type=jnp.float32)
                here = pl.ds(y_bit * width + t * tile, tile)
                out[:, here] = part if first else out[:, here] + part


def weight_sums_call(deltas, hidden, pieces, sums):
    rows, count = deltas.shape
    hid, width = hidden.shape[1], (pieces[0].shape[1] - LANES) // 2
    first = sums is None
    outs = (pltpu.VMEM((count, 2 * width), jnp.float32), pltpu.VMEM((hid, 2 * width), jnp.float32))
    held = () if first else tuple(near(sums))
    return pl.pallas_call(
        functools.partial(weight_sums_kernel, first, width),
        out_shape=outs,
        in_specs=[VMEM_WHOLE] * (18 + len(held)),
        out_specs=(VMEM_WHOLE,) * 2,
        scratch_shapes=[pltpu.VMEM((count + hid, rows), jnp.bfloat16)],
        input_output_aliases={} if first else {18: 0, 19: 1},
        compiler_params=pltpu.CompilerParams(vmem_limit_bytes=8 * 2**20),
        cost_estimate=pl.CostEstimate(
            flops=4 * (count + hid) * rows * width, transcendentals=0, bytes_accessed=4 * rows * width * 2
        ),
        name="weight_sums",
    )(*near((deltas, hidden)), *near(pieces), *held)


def column(row):
    return jnp.broadcast_to(row, (8, row.shape[1])).T[:, :1]


def soften_kernel(by_column, where_ref, *refs):
    count = len(by_column)
    grids, latents, scales = refs[:count], refs[count : 2 * count], refs[2 * count : 3 * count]
    outs = refs[3 * count : 5 * count]
    held, scale_s, sems = refs[5 * count :]
    mine = where_ref[1]
    width = outs[0].shape[1]
    loads = []
    for i in range(count):
        for y_bit in range(2):
            there = pl.ds(pl.multiple_of(jnp.bitwise_xor(mine, y_bit) * width, LANES), width)
            for k, src in enumerate((grids[i], latents[i])):
                loads.append(
                    pltpu.make_async_copy(src.at[:, there], held.at[i, y_bit, k], sems.at[i, y_bit, k])
                )
    for copy in loads:
        copy.start()
    for i in range(count):
        for y_bit in range(2):
            for copy in loads[4 * i + 2 * y_bit : 4 * i + 2 * y_bit + 2]:
                copy.wait()
            there = pl.ds(pl.multiple_of(jnp.bitwise_xor(mine, y_bit) * width, LANES), width)
            scale = scales[i][:, there] if by_column[i] else column(scales[i][...])
            if not by_column[i]:
                scale_s[...] = scale

            def rows_step(step, carry, i=i, y_bit=y_bit, scale=scale):
                rows = pl.ds(pl.multiple_of(step * STEP, STEP), STEP)
                soft = 0.5 * (1.0 + jnp.tanh(held[i, y_bit, 1, rows, :].astype(jnp.float32) / temper))
                level = held[i, y_bit, 0, rows, :].astype(jnp.float32) + soft
                here = scale if by_column[i] else scale_s[rows, :]
                outs[2 * i + y_bit][rows, :] = (level * here).astype(jnp.bfloat16)
                return carry

            lax.fori_loop(0, held.shape[3] // STEP, rows_step, 0)


def soften_call(where, grids, latents, scales, by_column):
    count = len(grids)
    hid, feat = grids[0].shape
    out = pltpu.VMEM((hid, feat // 2), jnp.bfloat16)
    return pl.pallas_call(
        functools.partial(soften_kernel, by_column),
        out_shape=(out,) * (2 * count),
        in_specs=[SMEM_WHOLE] + [HBM_WHOLE] * (2 * count) + [VMEM_WHOLE] * count,
        out_specs=(VMEM_WHOLE,) * (2 * count),
        scratch_shapes=[
            pltpu.VMEM((count, 2, 2, hid, feat // 2), jnp.bfloat16),
            pltpu.VMEM((hid, 1), jnp.float32),
            pltpu.SemaphoreType.DMA((count, 2, 2)),
        ],
        compiler_params=pltpu.CompilerParams(vmem_limit_bytes=12 * 2**20),
        cost_estimate=pl.CostEstimate(
            flops=5 * count * hid * feat,
            transcendentals=count * hid * feat,
            bytes_accessed=count * hid * feat * 6,
        ),
        name="soften",
    )(where, *away(grids), *away(latents), *scales)


def grads_kernel(where_ref, *refs):
    sums, latents, scales, outs = refs[0:2], refs[2:5], refs[5:8], refs[8:11]
    lats, stage, scale_s, lsems, osems = refs[11:]
    mine = where_ref[1]
    slots = stage.shape[0]
    hid, feat = latents[0].shape
    width, tile = feat // 2, stage.shape[2]
    lat_copies = [pltpu.make_async_copy(latents[i], lats.at[i], lsems.at[i]) for i in range(3)]
    for copy in lat_copies:
        copy.start()
    writes = []
    for i in range(2):
        scale_s[i] = column(scales[i][...])
    for i in range(3):
        lat_copies[i].wait()
        for y_bit in range(2):
            for t in range(width // tile):
                there = jnp.bitwise_xor(mine, y_bit) * width + t * tile
                there = pl.ds(pl.multiple_of(there, LANES), tile)
                here = pl.ds(y_bit * width + t * tile, tile)
                slot = len(writes) % slots
                if len(writes) >= slots:
                    writes[len(writes) - slots].wait()

                def rows_step(step, carry, i=i, slot=slot, here=here, there=there):
                    rows = pl.ds(pl.multiple_of(step * STEP, STEP), STEP)
                    slope = jnp.tanh(lats[i, rows, there].astype(jnp.float32) / temper)
                    scale = scales[i][:, there] if i == 2 else scale_s[i, rows, :]
                    factor = (grad_factor / (2.0 * temper)) * scale * (1.0 - slope * slope)
                    start = 0 if i == 2 else i * hid
                    total = sums[i // 2][pl.ds(pl.multiple_of(start + step * STEP, STEP), STEP), here]
                    stage[slot, rows, :] = total * factor
                    return carry

                lax.fori_loop(0, hid // STEP, rows_step, 0)
                copy = pltpu.make_async_copy(stage.at[slot], outs[i].at[:, there], osems.at[slot])
                copy.start()
                writes.append(copy)
    for copy in writes[-slots:]:
        copy.wait()


def grads_call(where, sums, latents, scales):
    hid, feat = latents[0].shape
    out = jax.ShapeDtypeStruct((hid, feat), jnp.float32)
    return pl.pallas_call(
        grads_kernel,
        out_shape=(out,) * 3,
        in_specs=[SMEM_WHOLE] + [VMEM_WHOLE] * 2 + [HBM_WHOLE] * 3 + [VMEM_WHOLE] * 3,
        out_specs=(HBM_WHOLE,) * 3,
        scratch_shapes=[
            pltpu.VMEM((3, hid, feat), jnp.bfloat16),
            pltpu.VMEM((6, hid, feat // 4), jnp.float32),
            pltpu.VMEM((2, hid, 1), jnp.float32),
            pltpu.SemaphoreType.DMA((3,)),
            pltpu.SemaphoreType.DMA((6,)),
        ],
        compiler_params=pltpu.CompilerParams(vmem_limit_bytes=12 * 2**20),
        cost_estimate=pl.CostEstimate(
            flops=18 * hid * feat,
            transcendentals=3 * hid * feat,
            bytes_accessed=3 * hid * feat * 6,
        ),
        name="latent_grads",
    )(where, *near(sums), *away(latents), *scales)


def pack_kernel(
    routes_hbm, weights_hbm, x_hbm, y_hbm, low_ref, high_ref, routes_ref, weights_ref, sems, small_sems
):
    tok_rows, width = x_hbm.shape
    half = tok_rows // 2
    small = [
        pltpu.make_async_copy(routes_hbm, routes_ref, small_sems.at[0]),
        pltpu.make_async_copy(weights_hbm, weights_ref, small_sems.at[1]),
    ]
    for copy in small:
        copy.start()
    copies = []
    for i, ref in enumerate((low_ref, high_ref)):
        for k, src in enumerate((x_hbm, y_hbm)):
            copies.append(
                pltpu.make_async_copy(
                    src.at[pl.ds(i * half, half), :],
                    ref.at[:, pl.ds(LANES + k * width, width)],
                    sems.at[i, k],
                )
            )
    for copy in copies:
        copy.start()
    for copy in small:
        copy.wait()
    lane = lax.broadcasted_iota(jnp.int32, (tok_rows, LANES), 1)
    routes, weights = routes_ref[...].T, weights_ref[...].astype(jnp.float32).T
    dense = jnp.zeros((tok_rows, LANES), jnp.float32)
    for k in range(routes.shape[1]):
        dense += jnp.where(lane == routes[:, k : k + 1], weights[:, k : k + 1], 0.0)
    dense = dense.astype(jnp.bfloat16)
    low_ref[:, :LANES] = dense[:half]
    high_ref[:, :LANES] = dense[half:]
    for copy in copies:
        copy.wait()


def pack_call(routes_t, weights_t, x, y):
    tok_rows, width = x.shape
    out = pltpu.VMEM((tok_rows // 2, LANES + 2 * width), jnp.bfloat16)
    return pl.pallas_call(
        pack_kernel,
        out_shape=(out, out),
        in_specs=[HBM_WHOLE] * 4,
        out_specs=(VMEM_WHOLE,) * 2,
        scratch_shapes=[
            pltpu.VMEM(routes_t.shape, routes_t.dtype),
            pltpu.VMEM(weights_t.shape, weights_t.dtype),
            pltpu.SemaphoreType.DMA((2, 2)),
            pltpu.SemaphoreType.DMA((2,)),
        ],
        compiler_params=pltpu.CompilerParams(vmem_limit_bytes=4 * 2**20),
        name="pack_tokens",
    )(*away((routes_t, weights_t, x, y)))


def final_kernel(groups, routes_ref, *refs):
    sums, (token_ref, route_ref) = refs[:groups], refs[groups:]
    total = sums[0][...].astype(jnp.float32)
    for ref in sums[1:]:
        total = total + ref[...].astype(jnp.float32)
    width = token_ref.shape[1]
    token_ref[...] = total[:, :width].astype(jnp.bfloat16)
    scores, routes = total[:, width:].T, routes_ref[...]
    row = lax.broadcasted_iota(jnp.int32, scores.shape, 0)
    for k in range(routes.shape[0]):
        chosen = jnp.where(row == routes[k : k + 1, :], scores, 0.0)
        route_ref[k : k + 1, :] = jnp.sum(chosen, axis=0, keepdims=True)


def final_call(routes_t, sums):
    tok_rows, cols = sums[0].shape
    return pl.pallas_call(
        functools.partial(final_kernel, len(sums)),
        out_shape=(
            jax.ShapeDtypeStruct((tok_rows, cols - LANES), jnp.bfloat16),
            jax.ShapeDtypeStruct(routes_t.shape, jnp.float32),
        ),
        in_specs=[VMEM_WHOLE] * (1 + len(sums)),
        out_specs=(VMEM_WHOLE,) * 2,
        compiler_params=pltpu.CompilerParams(vmem_limit_bytes=4 * 2**20),
        name="token_sum",
    )(routes_t, *near(sums))


def after(value, *deps):
    return lax.optimization_barrier((value, *deps))[0]


def dense_body(
    tokens,
    cotangent,
    route_weights,
    routes,
    grid_gate,
    latent_gate,
    scale_gate,
    grid_up,
    latent_up,
    scale_up,
    grid_down,
    latent_down,
    scale_down,
):
    n_ep = lax.axis_size("ep")
    where = jnp.stack([lax.axis_index("ep"), lax.axis_index("tp")]).astype(jnp.int32)
    hops = list(range(0, n_ep, 4))
    count = len(hops)
    halves = pack_call(routes.T, route_weights.T, tokens, cotangent)
    blocks = [halves]
    for g in range(1, count):
        held = (lambda piece: after(piece, blocks[-1][0])) if g == count - 1 and g > 1 else (lambda piece: piece)
        blocks.append([swap(held(piece), hops[g]) for piece in halves])
    parts = {}
    done, sums, planes = [], [], []

    def gather(g):
        low, high = blocks[g]
        low_x, high_y = swap(low, 2), swap(high, 0, 1)
        low_y, low_xy = swap(low, 0, 1), swap(low_x, 0, 1)
        high_x, high_xy = swap(high, 2), swap(high_y, 2)
        own = [low, low_x, low_y, low_xy, high, high_y, high_x, high_xy]
        parts[g] = own + [swap(piece, 1) for piece in own]

    gather(0)
    weights = list(soften_call(where, (grid_gate[0],), (latent_gate[0],), (scale_gate,), (False,)))
    late = after(where, parts[0][1])
    weights += soften_call(
        late,
        (grid_up[0], grid_down[0]),
        (latent_up[0], latent_down[0]),
        (scale_up, scale_down),
        (False, True),
    )
    for g in range(1, count):
        gather(g)
    weight_sums = None
    for g in range(count):
        done.append(group_call(where, parts[g], weights))
        swapped = swap(done[g][1], 1)
        sums.append(core_call(done[g][0], swapped))
        own, to_y, to_x, to_far = sums[g]
        got = (swap(to_y, 0, 1), swap(to_x, 2), swap(to_far, 2, 1))
        planes.append(plane_call(own, *got, jnp.bfloat16 if g else jnp.float32))
        weight_sums = weight_sums_call(done[g][2], done[g][3], parts[g], weight_sums)
    arrived = [planes[0]]
    for g in range(1, count):
        arrived.append(swap(planes[g], hops[g]))
    token_grad, route_grad = final_call(routes.T, arrived)
    grads = grads_call(
        where,
        weight_sums,
        (latent_gate[0], latent_up[0], latent_down[0]),
        (scale_gate, scale_up, scale_down),
    )
    return (*(grad[None] for grad in grads), token_grad, route_grad.T)


def dense_fits(mesh, routes, weight):
    n_ep, n_tp = mesh.shape["ep"], mesh.shape["tp"]
    experts = weight.shape[0]
    fits = n_tp == 2 and n_ep % 8 == 0 and (n_ep & (n_ep - 1)) == 0
    return fits and experts == n_ep and experts <= LANES and 2 * routes.shape[1] >= experts


def solution(mesh):
    specs = dict(
        mesh=mesh,
        in_specs=(
            P("ep", "tp"),
            P("ep", "tp"),
            P("ep", None),
            P("ep", None),
            P("ep", "tp", None),
            P("ep", "tp", None),
            P("ep", "tp"),
            P("ep", "tp", None),
            P("ep", "tp", None),
            P("ep", "tp"),
            P("ep", "tp", None),
            P("ep", "tp", None),
            P("ep", None),
        ),
        out_specs=(
            P("ep", "tp", None),
            P("ep", "tp", None),
            P("ep", "tp", None),
            P("ep", "tp"),
            P("ep", None),
        ),
        check_vma=False,
    )
    dense = jax.shard_map(dense_body, **specs)
    routed = jax.shard_map(routed_body, **specs)

    def program(*args):
        if not dense_fits(mesh, args[3], args[4]):
            return routed(*args)
        return dense(*args)

    return program
```
